256 devices in a mesh: section: 4 (over x_lo, core), row: 8 (over z), col: 8 (over x_hi, y).
Axes of the slice: x: 4 (x_hi: 2, x_lo: 2; x = x_hi * 2 + x_lo), y: 4, z: 8, core: 2. Of those that a mesh axis runs over, the one named last changes fastest.
Arguments:
- images: bfloat16 [4, 8, 80, 80, 512], P('section', None, 'row', 'col'), may hold values from -6 to 6
- block_in: bfloat16 [512, 256], replicated, may hold values from -0.25 to 0.25
- block_grouped_one: bfloat16 [1152, 256], replicated, may hold values from -0.1875 to 0.1875
- block_grouped_two: bfloat16 [1152, 256], replicated, may hold values from -0.1875 to 0.1875
- block_out: bfloat16 [256, 512], replicated, may hold values from -0.375 to 0.375
- trans_in: bfloat16 [512, 768], replicated, may hold values from -0.25 to 0.25
- trans_grouped_one: bfloat16 [1152, 768], replicated, may hold values from -0.1875 to 0.1875
- trans_grouped_two: bfloat16 [1152, 768], replicated, may hold values from -0.1875 to 0.1875
- trans_out: bfloat16 [768, 1536], replicated, may hold values from -0.21875 to 0.21875
- trans_short: bfloat16 [512, 1536], replicated, may hold values from -0.25 to 0.25
Outputs:
- features: bfloat16 [4, 8, 40, 40, 1536], P('section', 'row', 'col')
The draws below stay inside these ranges and needn't reach their ends.
All inputs are finite; a program needn't handle non-finite values.
Results may differ from the reference program's by a relative error of at most 0.012.
Values may be sent and summed in bfloat16 or wider, within the bound.
A program may use at most 64 MiB of HBM per device.

```python
import jax
import jax.numpy as jnp
from jax import lax

WIDE_TWO = 512
MID_TWO = 256
WIDE_THREE = 1536
MID_THREE = 768
GROUP = 128
SIDE = 80
IMG = 8
LOTS = 4


def shard_levels(rng, extent, cuts, least, largest):
    loudness = 1.0
    for dim, blocks in cuts:
        draws = jax.random.uniform(jax.random.fold_in(jax.random.fold_in(rng, 6), dim), (blocks,), jnp.float32, least / len(cuts), largest / len(cuts))
        loudness = loudness * jnp.repeat(jnp.exp(draws), extent[dim] // blocks).reshape((-1,) + (1,) * (len(extent) - 1 - dim))
    return loudness


def normal_values(key, dims, spread, reach, pieces=(), dtype=jnp.bfloat16):
    entries = jax.random.normal(key, dims, jnp.float32) * spread
    if len(pieces) > 0:
        entries = shard_levels(key, dims, pieces, -0.22, 0.18) * entries
    return jnp.clip(entries, min=-reach, max=reach).astype(dtype)


def setup_inputs(seed: int = 0) -> dict:
    key_list = jax.random.split(jax.random.key(seed), 11)
    images = normal_values(key_list[0], (LOTS, IMG, SIDE, SIDE, WIDE_TWO), 1.0, 6.0, ((0, 4), (2, 8), (3, 8)))
    block_in = normal_values(key_list[1], (WIDE_TWO, MID_TWO), WIDE_TWO ** -0.5, 0.25)
    block_grouped_one = normal_values(key_list[2], (9 * GROUP, MID_TWO), (9 * GROUP) ** -0.5, 0.1875)
    block_grouped_two = normal_values(key_list[3], (9 * GROUP, MID_TWO), (9 * GROUP) ** -0.5, 0.1875)
    block_out = normal_values(key_list[4], (MID_TWO, WIDE_TWO), MID_TWO ** -0.5, 0.375)
    trans_in = normal_values(key_list[5], (WIDE_TWO, MID_THREE), WIDE_TWO ** -0.5, 0.25)
    trans_grouped_one = normal_values(key_list[6], (9 * GROUP, MID_THREE), (9 * GROUP) ** -0.5, 0.1875)
    trans_grouped_two = normal_values(key_list[7], (9 * GROUP, MID_THREE), (9 * GROUP) ** -0.5, 0.1875)
    trans_out = normal_values(key_list[8], (MID_THREE, WIDE_THREE), MID_THREE ** -0.5, 0.21875)
    trans_short = normal_values(key_list[9], (WIDE_TWO, WIDE_THREE), WIDE_TWO ** -0.5, 0.25)
    return dict(images=images, block_in=block_in, block_grouped_one=block_grouped_one, block_grouped_two=block_grouped_two, block_out=block_out, trans_in=trans_in, trans_grouped_one=trans_grouped_one, trans_grouped_two=trans_grouped_two, trans_out=trans_out, trans_short=trans_short)


GELU_GAIN = 1.7015
RESIDUAL_SCALE = 0.2
BETA_BLOCK = 0.9805
BETA_TRANSITION = 0.9623


def activate(values):
    return GELU_GAIN * jax.nn.gelu(values, approximate=True)


def pad_sides(tensor):
    return jnp.pad(tensor, ((0, 0), (1, 1), (1, 1), (0, 0)))


def matmul_rows(tensor, weight):
    shaped = tensor.shape
    result = jnp.dot(tensor.reshape(-1, shaped[-1]), weight, preferred_element_type=jnp.float32)
    return result.reshape(shaped[:-1] + (weight.shape[1],))


def group_conv(padded, weight, stride):
    batches, height, breadth, channels = padded.shape
    group_width = weight.shape[0] // 9
    out_height = (height - 2) // stride
    out_breadth = (breadth - 2) // stride
    offset = stride - 1
    tap_list = []
    for row_tap in range(3):
        for col_tap in range(3):
            start_row = offset + row_tap
            start_col = offset + col_tap
            tap_list.append(lax.slice(padded, (0, start_row, start_col, 0),
                                      (batches, start_row + stride * (out_height - 1) + 1,
                                       start_col + stride * (out_breadth - 1) + 1, channels),
                                      (1, stride, stride, 1)))
    stacked = jnp.stack(tap_list, axis=3)
    groups = channels // group_width
    stacked = stacked.reshape(batches, out_height, out_breadth, 9, groups, group_width)
    kernel = weight.reshape(9, group_width, groups, group_width)
    result = jnp.einsum("nhwtgc,tcgd->nhwgd", stacked.astype(jnp.float32), kernel.astype(jnp.float32))
    return result.reshape(batches, out_height, out_breadth, channels)


def reference(images, block_in, block_grouped_one, block_grouped_two, block_out,
              trans_in, trans_grouped_one, trans_grouped_two, trans_out, trans_short):
    lot_count, image_count, height, breadth, channels = images.shape
    flat = images.reshape(lot_count * image_count, height, breadth, channels)

    def one_image(single):
        source = single[None]
        pre_block = (activate(source.astype(jnp.float32)) * BETA_BLOCK).astype(jnp.bfloat16)
        first_mid = activate(matmul_rows(pre_block, block_in)).astype(jnp.bfloat16)
        second_mid = activate(group_conv(pad_sides(first_mid), block_grouped_one, 1)).astype(jnp.bfloat16)
        third_mid = activate(group_conv(pad_sides(second_mid), block_grouped_two, 1)).astype(jnp.bfloat16)
        block_result = (source.astype(jnp.float32) + RESIDUAL_SCALE * matmul_rows(third_mid, block_out)).astype(jnp.bfloat16)
        pre_trans = (activate(block_result.astype(jnp.float32)) * BETA_TRANSITION).astype(jnp.bfloat16)
        pooled = pre_trans.astype(jnp.float32).reshape(1, height // 2, 2, breadth // 2, 2, channels)
        pooled = jnp.mean(pooled, axis=(2, 4)).astype(jnp.bfloat16)
        trans_first = activate(matmul_rows(pre_trans, trans_in)).astype(jnp.bfloat16)
        trans_second = activate(group_conv(pad_sides(trans_first), trans_grouped_one, 2)).astype(jnp.bfloat16)
        trans_third = activate(group_conv(pad_sides(trans_second), trans_grouped_two, 1)).astype(jnp.bfloat16)
        result = matmul_rows(pooled, trans_short) + RESIDUAL_SCALE * matmul_rows(trans_third, trans_out)
        return result.astype(jnp.bfloat16)[0]

    outputs = lax.map(one_image, flat)
    return outputs.reshape(lot_count, image_count, height // 2, breadth // 2, outputs.shape[-1])
```

```python
import functools

import jax
import jax.numpy as jnp
from jax import lax
from jax.experimental import pallas as pl
from jax.experimental.pallas import tpu as pltpu
from jax.sharding import PartitionSpec as P

GELU_GAIN = 1.7015
RESIDUAL_SCALE = 0.2
BETA_BLOCK = 0.9805
BETA_TRANSITION = 0.9623
GROUP = 128
MESH = pl.DeviceIdType.MESH

TOP = 4
BOTTOM = 5


def activate(values):
    return GELU_GAIN * jax.nn.gelu(values, approximate=True)


def gather_kernel(nrow, ncol, img_ref, out_ref, send_sem, recv_sem):
    s = lax.axis_index("section")
    r = lax.axis_index("row")
    c = lax.axis_index("col")
    n_img, th, tw = img_ref.shape[0], img_ref.shape[1], img_ref.shape[2]
    barrier = pltpu.get_barrier_semaphore()

    dests = []
    for i in range(n_img):
        for k, delta in enumerate((-1, 0, 1)):
            valid = jnp.logical_and(r + delta >= 0, r + delta < ncol)
            cd = lax.rem(r + delta + ncol, ncol)
            is_self = jnp.logical_and(r == i, cd == c)
            dests.append((i, k, delta, cd, valid, is_self))
    sources = []
    for d in range(3):
        for cs in range(ncol):
            valid = jnp.logical_and(c + d - 1 >= 0, c + d - 1 < nrow)
            rs = lax.rem(c + d - 1 + nrow, nrow)
            is_self = jnp.logical_and(rs == r, cs == c)
            sources.append((d, cs, rs, valid, is_self))

    def remote(valid, is_self):
        return jnp.logical_and(valid, jnp.logical_not(is_self))

    for i, k, delta, cd, valid, is_self in dests:
        @pl.when(remote(valid, is_self))
        def _():
            pl.semaphore_signal(barrier, 1, device_id=(s, i, cd), device_id_type=MESH)
    for d, cs, rs, valid, is_self in sources:
        @pl.when(remote(valid, is_self))
        def _():
            pl.semaphore_signal(barrier, 1, device_id=(s, rs, cs), device_id_type=MESH)
    peers = [remote(valid, is_self) for _, _, _, _, valid, is_self in dests]
    peers += [remote(valid, is_self) for _, _, _, valid, is_self in sources]
    pl.semaphore_wait(barrier, sum(p.astype(jnp.int32) for p in peers))

    spans = {0: (0, th, TOP), 1: (th - TOP, TOP, 0), -1: (0, BOTTOM, TOP + th)}
    remote_copies = []
    for i, k, delta, cd, valid, is_self in dests:
        r0, n, d0 = spans[delta]
        src = img_ref.at[i, pl.ds(r0, n)]
        dst = out_ref.at[pl.ds(d0, n), c]
        slot = 1 - delta
        rdesc = pltpu.make_async_remote_copy(
            src_ref=src,
            dst_ref=dst,
            send_sem=send_sem.at[i, k],
            recv_sem=recv_sem.at[slot, c],
            device_id=(s, i, cd),
            device_id_type=MESH,
        )
        ldesc = pltpu.make_async_copy(src, dst, recv_sem.at[slot, c])
        is_remote = remote(valid, is_self)

        @pl.when(is_remote)
        def _():
            rdesc.start()

        @pl.when(jnp.logical_and(valid, is_self))
        def _():
            ldesc.start()

        remote_copies.append((rdesc, is_remote))

    lands = {0: (TOP, 0), 1: (th, TOP), 2: (BOTTOM, TOP + th)}
    for d, cs, rs, valid, is_self in sources:
        n, d0 = lands[d]
        dst = out_ref.at[pl.ds(d0, n), cs]
        desc = pltpu.make_async_copy(dst, dst, recv_sem.at[d, cs])

        @pl.when(valid)
        def _():
            desc.wait()

    for rdesc, is_remote in remote_copies:
        @pl.when(is_remote)
        def _():
            rdesc.wait_send()


def gather_strips(tiles, nrow, ncol):
    n_img, th, tw, ch = tiles.shape
    return pl.pallas_call(
        functools.partial(gather_kernel, nrow, ncol),
        out_shape=jax.ShapeDtypeStruct((TOP + th + BOTTOM, ncol, tw, ch), tiles.dtype),
        in_specs=[pl.BlockSpec(memory_space=pl.ANY)],
        out_specs=pl.BlockSpec(memory_space=pl.ANY),
        scratch_shapes=[
            pltpu.SemaphoreType.DMA((n_img, 3)),
            pltpu.SemaphoreType.DMA((3, ncol)),
        ],
        compiler_params=pltpu.CompilerParams(collective_id=0, has_side_effects=True),
    )(tiles)


def matmul_rows(tensor, weight):
    shaped = tensor.shape
    result = jnp.dot(tensor.reshape(-1, shaped[-1]), weight, preferred_element_type=jnp.float32)
    return result.reshape(shaped[:-1] + (weight.shape[1],))


def group_conv(tensor, weight, stride, col_pad):
    channels = tensor.shape[-1]
    kernel = weight.reshape(3, 3, GROUP, channels)
    return lax.conv_general_dilated(
        tensor,
        kernel,
        window_strides=(stride, stride),
        padding=((0, 0), col_pad),
        dimension_numbers=("NHWC", "HWIO", "NHWC"),
        feature_group_count=channels // GROUP,
        preferred_element_type=jnp.float32,
    )


def keep_rows(tensor, first, height):
    rows = first + lax.broadcasted_iota(jnp.int32, (1, tensor.shape[1], 1, 1), 1)
    inside = jnp.logical_and(rows >= 0, rows < height)
    return jnp.where(inside, tensor, jnp.zeros_like(tensor))


def local(
    images,
    block_in,
    block_grouped_one,
    block_grouped_two,
    block_out,
    trans_in,
    trans_grouped_one,
    trans_grouped_two,
    trans_out,
    trans_short,
):
    nrow = lax.axis_size("row")
    ncol = lax.axis_size("col")
    _, n_img, th, tw, ch = images.shape
    height = th * nrow
    c = lax.axis_index("col")
    base = c * th - TOP

    strip = gather_strips(images.reshape(n_img, th, tw, ch), nrow, ncol)
    strip = strip.reshape(1, TOP + th + BOTTOM, ncol * tw, ch)
    pre_block = (activate(strip.astype(jnp.float32)) * BETA_BLOCK).astype(jnp.bfloat16)
    first_mid = activate(matmul_rows(pre_block, block_in)).astype(jnp.bfloat16)
    first_mid = keep_rows(first_mid, base, height)
    second_mid = activate(group_conv(first_mid, block_grouped_one, 1, (1, 1))).astype(jnp.bfloat16)
    second_mid = keep_rows(second_mid, base + 1, height)
    third_mid = activate(group_conv(second_mid, block_grouped_two, 1, (1, 1))).astype(jnp.bfloat16)
    block_result = (
        strip[:, 2:-2].astype(jnp.float32) + RESIDUAL_SCALE * matmul_rows(third_mid, block_out)
    ).astype(jnp.bfloat16)

    pre_trans = (activate(block_result.astype(jnp.float32)) * BETA_TRANSITION).astype(jnp.bfloat16)
    core = pre_trans[:, TOP - 2 : TOP - 2 + th]
    width = core.shape[2]
    pooled = core.astype(jnp.float32).reshape(1, th // 2, 2, width // 2, 2, ch)
    pooled = jnp.mean(pooled, axis=(2, 4)).astype(jnp.bfloat16)
    trans_first = activate(matmul_rows(pre_trans, trans_in)).astype(jnp.bfloat16)
    trans_first = keep_rows(trans_first, base + 2, height)
    trans_second = activate(group_conv(trans_first, trans_grouped_one, 2, (0, 1))).astype(jnp.bfloat16)
    trans_second = keep_rows(trans_second, c * (th // 2) - 1, height // 2)
    trans_third = activate(group_conv(trans_second, trans_grouped_two, 1, (1, 1))).astype(jnp.bfloat16)
    result = matmul_rows(pooled, trans_short) + RESIDUAL_SCALE * matmul_rows(trans_third, trans_out)
    return result.astype(jnp.bfloat16)[None]


def solution(mesh):
    in_specs = (P("section", None, "row", "col", None), P(), P(), P(), P(), P(), P(), P(), P(), P())
    out_specs = P("section", "row", "col", None, None)
    return jax.shard_map(local, mesh=mesh, in_specs=in_specs, out_specs=out_specs, check_vma=False)
```

```python
import functools

import jax
import jax.numpy as jnp
from jax import lax
from jax.experimental import pallas as pl
from jax.experimental.pallas import tpu as pltpu
from jax.sharding import PartitionSpec as P

GELU_GAIN = 1.7015
RESIDUAL_SCALE = 0.2
BETA_BLOCK = 0.9805
BETA_TRANSITION = 0.9623
GROUP = 128
MESH = pl.DeviceIdType.MESH

TOP = 4
BOTTOM = 5


def activate(values):
    return GELU_GAIN * jax.nn.gelu(values, approximate=True)


def gather_kernel(nrow, ncol, img_ref, out_ref, send_sem, recv_sem):
    s = lax.axis_index("section")
    r = lax.axis_index("row")
    c = lax.axis_index("col")
    n_img, th, tw = img_ref.shape[0], img_ref.shape[1], img_ref.shape[2]
    barrier = pltpu.get_barrier_semaphore()

    dests = []
    for i in range(n_img):
        for k, delta in enumerate((-1, 0, 1)):
            valid = jnp.logical_and(r + delta >= 0, r + delta < ncol)
            cd = lax.rem(r + delta + ncol, ncol)
            is_self = jnp.logical_and(r == i, cd == c)
            dests.append((i, k, delta, cd, valid, is_self))
    sources = []
    for d in range(3):
        for cs in range(ncol):
            valid = jnp.logical_and(c + d - 1 >= 0, c + d - 1 < nrow)
            rs = lax.rem(c + d - 1 + nrow, nrow)
            is_self = jnp.logical_and(rs == r, cs == c)
            sources.append((d, cs, rs, valid, is_self))

    def remote(valid, is_self):
        return jnp.logical_and(valid, jnp.logical_not(is_self))

    for i, k, delta, cd, valid, is_self in dests:
        @pl.when(remote(valid, is_self))
        def _():
            pl.semaphore_signal(barrier, 1, device_id=(s, i, cd), device_id_type=MESH)
    for d, cs, rs, valid, is_self in sources:
        @pl.when(remote(valid, is_self))
        def _():
            pl.semaphore_signal(barrier, 1, device_id=(s, rs, cs), device_id_type=MESH)
    peers = [remote(valid, is_self) for _, _, _, _, valid, is_self in dests]
    peers += [remote(valid, is_self) for _, _, _, valid, is_self in sources]
    pl.semaphore_wait(barrier, sum(p.astype(jnp.int32) for p in peers))

    spans = {0: (0, th, TOP), 1: (th - TOP, TOP, 0), -1: (0, BOTTOM, TOP + th)}
    remote_copies = []
    for i, k, delta, cd, valid, is_self in dests:
        r0, n, d0 = spans[delta]
        src = img_ref.at[i, pl.ds(r0, n)]
        dst = out_ref.at[pl.ds(d0, n), c]
        slot = 1 - delta
        rdesc = pltpu.make_async_remote_copy(
            src_ref=src,
            dst_ref=dst,
            send_sem=send_sem.at[i, k],
            recv_sem=recv_sem.at[slot, c],
            device_id=(s, i, cd),
            device_id_type=MESH,
        )
        ldesc = pltpu.make_async_copy(src, dst, recv_sem.at[slot, c])
        is_remote = remote(valid, is_self)

        @pl.when(is_remote)
        def _():
            rdesc.start()

        @pl.when(jnp.logical_and(valid, is_self))
        def _():
            ldesc.start()

        remote_copies.append((rdesc, is_remote))

    lands = {0: (TOP, 0), 1: (th, TOP), 2: (BOTTOM, TOP + th)}
    for d, cs, rs, valid, is_self in sources:
        n, d0 = lands[d]
        dst = out_ref.at[pl.ds(d0, n), cs]
        desc = pltpu.make_async_copy(dst, dst, recv_sem.at[d, cs])

        @pl.when(valid)
        def _():
            desc.wait()

    for rdesc, is_remote in remote_copies:
        @pl.when(is_remote)
        def _():
            rdesc.wait_send()


def gather_strips(tiles, nrow, ncol):
    n_img, th, tw, ch = tiles.shape
    return pl.pallas_call(
        functools.partial(gather_kernel, nrow, ncol),
        out_shape=jax.ShapeDtypeStruct((TOP + th + BOTTOM, ncol, tw, ch), tiles.dtype),
        in_specs=[pl.BlockSpec(memory_space=pl.ANY)],
        out_specs=pl.BlockSpec(memory_space=pl.ANY),
        scratch_shapes=[
            pltpu.SemaphoreType.DMA((n_img, 3)),
            pltpu.SemaphoreType.DMA((3, ncol)),
        ],
        compiler_params=pltpu.CompilerParams(collective_id=0, has_side_effects=True),
    )(tiles)


def tap_weights(weight):
    channels = weight.shape[1]
    return weight.reshape(3, 3, GROUP, channels).transpose(1, 0, 2, 3).reshape(3, 3 * GROUP, channels)


def inside_rows(count, width, first, height):
    rows = first + lax.broadcasted_iota(jnp.int32, (count * width, 1), 0) // width
    return jnp.logical_and(rows >= 0, rows < height)


def column_of(count, width):
    return lax.broadcasted_iota(jnp.int32, (count * width, 1), 0) % width


def conv_taps(rows_of, out_rows, width, w_ref, group):
    sl = slice(group * GROUP, (group + 1) * GROUP)
    slab = jnp.concatenate([rows_of(a)[:, :, sl] for a in range(3)], axis=-1)
    slab = slab.reshape(out_rows * width, 3 * GROUP).astype(jnp.bfloat16)
    return [jnp.dot(slab, w_ref[b, :, sl], preferred_element_type=jnp.float32) for b in range(3)]


def conv_same(x, w_ref):
    in_rows, width, channels = x.shape
    out_rows = in_rows - 2
    n = out_rows * width
    col = column_of(out_rows, width)
    outs = []
    for g in range(channels // GROUP):
        y = conv_taps(lambda a: x[a : a + out_rows], out_rows, width, w_ref, g)
        left = jnp.where(col == 0, 0.0, pltpu.roll(y[0], 1, 0))
        right = jnp.where(col == width - 1, 0.0, pltpu.roll(y[2], n - 1, 0))
        outs.append(y[1] + left + right)
    return jnp.concatenate(outs, axis=-1)


def block_kernel(base_ref, x_ref, win_ref, w1_ref, w2_ref, wout_ref, o_ref):
    rows, width, ch = x_ref.shape
    height = base_ref[1]
    base = base_ref[0]
    x = x_ref[...].astype(jnp.float32).reshape(rows * width, ch)
    pre = (activate(x) * BETA_BLOCK).astype(jnp.bfloat16)
    first = activate(jnp.dot(pre, win_ref[...], preferred_element_type=jnp.float32))
    first = jnp.where(inside_rows(rows, width, base, height), first, 0.0)
    first = first.astype(jnp.bfloat16).astype(jnp.float32).reshape(rows, width, -1)
    second = activate(conv_same(first, w1_ref))
    second = jnp.where(inside_rows(rows - 2, width, base + 1, height), second, 0.0)
    second = second.astype(jnp.bfloat16).astype(jnp.float32).reshape(rows - 2, width, -1)
    third = activate(conv_same(second, w2_ref)).astype(jnp.bfloat16)
    skip = x_ref[2 : rows - 2].astype(jnp.float32).reshape((rows - 4) * width, ch)
    out = skip + RESIDUAL_SCALE * jnp.dot(third, wout_ref[...], preferred_element_type=jnp.float32)
    o_ref[...] = out.astype(o_ref.dtype).reshape(rows - 4, width, ch)


def trans_kernel(base_ref, x_ref, win_ref, w1_ref, w2_ref, wout_ref, wshort_ref, o_ref, pool_scr, sub_scr):
    rows, width, ch = x_ref.shape
    core_rows = rows - 5
    half = width // 2
    height = base_ref[1]
    base = base_ref[0] + 2
    x = x_ref[...].astype(jnp.float32).reshape(rows * width, ch)
    pre = (activate(x) * BETA_TRANSITION).astype(jnp.bfloat16)

    core = pre.astype(jnp.float32).reshape(rows, width, ch)[2 : 2 + core_rows]
    core = core.reshape(core_rows // 2, 2, width, ch)
    summed = (core[:, 0] + core[:, 1]).reshape(core_rows // 2 * width, ch)
    n_pool = core_rows // 2 * half
    parts = []
    for k in range(ch // GROUP):
        pool_scr[k] = summed[:, k * GROUP : (k + 1) * GROUP]
        part = pool_scr.at[k]
        parts.append(part[pl.ds(0, n_pool, stride=2), :] + part[pl.ds(1, n_pool, stride=2), :])
    pooled = (jnp.concatenate(parts, axis=-1) * 0.25).astype(jnp.bfloat16)

    first = activate(jnp.dot(pre, win_ref[...], preferred_element_type=jnp.float32))
    first = jnp.where(inside_rows(rows, width, base, height), first, 0.0)
    first = first.astype(jnp.bfloat16).astype(jnp.float32).reshape(rows, width, -1)
    mid = first.shape[-1]
    first = jnp.concatenate([first, jnp.zeros((1, width, mid), jnp.float32)], axis=0)
    pairs = first.reshape((rows + 1) // 2, 2, width, mid)
    out_rows = (rows - 1) // 2
    picks = (pairs[:out_rows, 0], pairs[:out_rows, 1], pairs[1 : out_rows + 1, 0])
    n = out_rows * width
    col = column_of(out_rows, width)
    for g in range(mid // GROUP):
        y = conv_taps(lambda a: picks[a], out_rows, width, w1_ref, g)
        z = y[0] + pltpu.roll(y[1], n - 1, 0) + jnp.where(col >= width - 2, 0.0, pltpu.roll(y[2], n - 2, 0))
        sub_scr[g, pl.ds(0, n), :] = z
    picked = [sub_scr.at[g][pl.ds(0, out_rows * half, stride=2), :] for g in range(mid // GROUP)]
    second = activate(jnp.concatenate(picked, axis=-1))
    second = jnp.where(inside_rows(out_rows, half, base_ref[0] // 2 + 1, height // 2), second, 0.0)
    second = second.astype(jnp.bfloat16).astype(jnp.float32).reshape(out_rows, half, mid)
    third = activate(conv_same(second, w2_ref)).astype(jnp.bfloat16)
    out = jnp.dot(pooled, wshort_ref[...], preferred_element_type=jnp.float32)
    out = out + RESIDUAL_SCALE * jnp.dot(third, wout_ref[...], preferred_element_type=jnp.float32)
    o_ref[...] = out.astype(o_ref.dtype)


def vmem_call(kernel, out_shape, n_in, scratch=()):
    return pl.pallas_call(
        kernel,
        out_shape=out_shape,
        in_specs=[pl.BlockSpec(memory_space=pltpu.SMEM)] + [pl.BlockSpec(memory_space=pltpu.VMEM)] * n_in,
        out_specs=pl.BlockSpec(memory_space=pltpu.VMEM),
        scratch_shapes=list(scratch),
    )


def compute(strip, base_info, block_in, block_grouped_one, block_grouped_two, block_out,
            trans_in, trans_grouped_one, trans_grouped_two, trans_out, trans_short):
    rows, width, ch = strip.shape
    block_result = vmem_call(block_kernel, jax.ShapeDtypeStruct((rows - 4, width, ch), jnp.bfloat16), 5)(
        base_info, strip, block_in, tap_weights(block_grouped_one), tap_weights(block_grouped_two), block_out
    )
    t_rows = rows - 4
    core_rows = t_rows - 5
    out_rows = (t_rows - 1) // 2
    mid = trans_in.shape[1]
    wide = trans_out.shape[1]
    scratch = (
        pltpu.VMEM((ch // GROUP, core_rows // 2 * width, GROUP), jnp.float32),
        pltpu.VMEM((mid // GROUP, out_rows * width + 8, GROUP), jnp.float32),
    )
    out_shape = jax.ShapeDtypeStruct(((core_rows // 2) * (width // 2), wide), jnp.bfloat16)
    features = vmem_call(trans_kernel, out_shape, 6, scratch)(
        base_info, block_result, trans_in, tap_weights(trans_grouped_one), tap_weights(trans_grouped_two),
        trans_out, trans_short
    )
    return features.reshape(core_rows // 2, width // 2, wide)


def local(
    images,
    block_in,
    block_grouped_one,
    block_grouped_two,
    block_out,
    trans_in,
    trans_grouped_one,
    trans_grouped_two,
    trans_out,
    trans_short,
):
    nrow = lax.axis_size("row")
    ncol = lax.axis_size("col")
    _, n_img, th, tw, ch = images.shape
    c = lax.axis_index("col")
    base_info = jnp.stack([c * th - TOP, th * nrow]).astype(jnp.int32)
    strip = gather_strips(images.reshape(n_img, th, tw, ch), nrow, ncol)
    strip = strip.reshape(TOP + th + BOTTOM, ncol * tw, ch)
    features = compute(strip, base_info, block_in, block_grouped_one, block_grouped_two, block_out,
                       trans_in, trans_grouped_one, trans_grouped_two, trans_out, trans_short)
    return features[None, None]


def solution(mesh):
    in_specs = (P("section", None, "row", "col", None), P(), P(), P(), P(), P(), P(), P(), P(), P())
    out_specs = P("section", "row", "col", None, None)
    return jax.shard_map(local, mesh=mesh, in_specs=in_specs, out_specs=out_specs, check_vma=False)
```

```python
import functools

import jax
import jax.numpy as jnp
from jax import lax
from jax.experimental import pallas as pl
from jax.experimental.pallas import tpu as pltpu
from jax.sharding import PartitionSpec as P

GELU_GAIN = 1.7015
RESIDUAL_SCALE = 0.2
BETA_BLOCK = 0.9805
BETA_TRANSITION = 0.9623
GROUP = 128
MESH = pl.DeviceIdType.MESH

TOP = 4
BOTTOM = 5


def activate(values):
    return GELU_GAIN * jax.nn.gelu(values, approximate=True)


def gather_kernel(nrow, ncol, img_ref, out_ref, send_sem, recv_sem, fwd_send, fwd_recv):
    s = lax.axis_index("section")
    r = lax.axis_index("row")
    c = lax.axis_index("col")
    n_img, th, tw = img_ref.shape[0], img_ref.shape[1], img_ref.shape[2]
    barrier = pltpu.get_barrier_semaphore()

    dests = []
    for i in range(n_img):
        is_self = jnp.logical_and(r == i, r == c)
        dests.append((i, jnp.logical_not(is_self), is_self))
    sources = []
    for cs in range(ncol):
        is_self = jnp.logical_and(c == r, cs == c)
        sources.append((cs, jnp.logical_not(is_self)))
    up = c - 1
    down = c + 1
    has_up = up >= 0
    has_down = down < ncol
    up_id = (s, r, lax.rem(up + ncol, ncol))
    down_id = (s, r, lax.rem(down, ncol))

    for i, is_remote, _ in dests:
        @pl.when(is_remote)
        def _():
            pl.semaphore_signal(barrier, 1, device_id=(s, i, r), device_id_type=MESH)
    for cs, is_remote in sources:
        @pl.when(is_remote)
        def _():
            pl.semaphore_signal(barrier, 1, device_id=(s, c, cs), device_id_type=MESH)
    for flag, dev in ((has_up, up_id), (has_down, down_id)):
        @pl.when(flag)
        def _():
            pl.semaphore_signal(barrier, 1, device_id=dev, device_id_type=MESH)
    peers = [p for _, p, _ in dests] + [p for _, p in sources] + [has_up, has_down]
    pl.semaphore_wait(barrier, sum(p.astype(jnp.int32) for p in peers))

    remote_copies = []
    for i, is_remote, is_self in dests:
        src = img_ref.at[i]
        dst = out_ref.at[pl.ds(TOP, th), c]
        rdesc = pltpu.make_async_remote_copy(
            src_ref=src,
            dst_ref=dst,
            send_sem=send_sem.at[i],
            recv_sem=recv_sem.at[c],
            device_id=(s, i, r),
            device_id_type=MESH,
        )
        ldesc = pltpu.make_async_copy(src, dst, recv_sem.at[c])

        @pl.when(is_remote)
        def _():
            rdesc.start()

        @pl.when(is_self)
        def _():
            ldesc.start()

        remote_copies.append((rdesc, is_remote))

    for cs, _ in sources:
        dst = out_ref.at[pl.ds(TOP, th), cs]
        pltpu.make_async_copy(dst, dst, recv_sem.at[cs]).wait()

    to_up = pltpu.make_async_remote_copy(
        src_ref=out_ref.at[pl.ds(TOP, BOTTOM)],
        dst_ref=out_ref.at[pl.ds(TOP + th, BOTTOM)],
        send_sem=fwd_send.at[0],
        recv_sem=fwd_recv.at[1],
        device_id=up_id,
        device_id_type=MESH,
    )
    to_down = pltpu.make_async_remote_copy(
        src_ref=out_ref.at[pl.ds(TOP + th - TOP, TOP)],
        dst_ref=out_ref.at[pl.ds(0, TOP)],
        send_sem=fwd_send.at[1],
        recv_sem=fwd_recv.at[0],
        device_id=down_id,
        device_id_type=MESH,
    )

    @pl.when(has_up)
    def _():
        to_up.start()

    @pl.when(has_down)
    def _():
        to_down.start()

    @pl.when(has_down)
    def _():
        pltpu.make_async_copy(to_up.dst_ref, to_up.dst_ref, fwd_recv.at[1]).wait()

    @pl.when(has_up)
    def _():
        pltpu.make_async_copy(to_down.dst_ref, to_down.dst_ref, fwd_recv.at[0]).wait()

    for rdesc, is_remote in remote_copies:
        @pl.when(is_remote)
        def _():
            rdesc.wait_send()

    @pl.when(has_up)
    def _():
        to_up.wait_send()

    @pl.when(has_down)
    def _():
        to_down.wait_send()


def gather_strips(tiles, nrow, ncol):
    n_img, th, tw, ch = tiles.shape
    return pl.pallas_call(
        functools.partial(gather_kernel, nrow, ncol),
        out_shape=jax.ShapeDtypeStruct((TOP + th + BOTTOM, ncol, tw, ch), tiles.dtype),
        in_specs=[pl.BlockSpec(memory_space=pl.ANY)],
        out_specs=pl.BlockSpec(memory_space=pl.ANY),
        scratch_shapes=[
            pltpu.SemaphoreType.DMA((n_img,)),
            pltpu.SemaphoreType.DMA((ncol,)),
            pltpu.SemaphoreType.DMA((2,)),
            pltpu.SemaphoreType.DMA((2,)),
        ],
        compiler_params=pltpu.CompilerParams(collective_id=0, has_side_effects=True),
    )(tiles)


def inside_rows(count, width, first, height):
    rows = first + lax.broadcasted_iota(jnp.int32, (count * width, 1), 0) // width
    return jnp.logical_and(rows >= 0, rows < height)


def column_of(count, width):
    return lax.broadcasted_iota(jnp.int32, (count * width, 1), 0) % width


def conv_taps(rows_of, out_rows, width, w_ref, group):
    sl = slice(group * GROUP, (group + 1) * GROUP)
    slab = jnp.concatenate([rows_of(a)[:, :, sl] for a in range(3)], axis=-1)
    slab = slab.reshape(out_rows * width, 3 * GROUP).astype(jnp.bfloat16)
    outs = []
    for b in range(3):
        taps = jnp.concatenate([w_ref[(3 * a + b) * GROUP : (3 * a + b + 1) * GROUP, sl] for a in range(3)], axis=0)
        outs.append(jnp.dot(slab, taps, preferred_element_type=jnp.float32))
    return outs


def conv_same(x, w_ref):
    in_rows, width, channels = x.shape
    out_rows = in_rows - 2
    n = out_rows * width
    col = column_of(out_rows, width)
    outs = []
    for g in range(channels // GROUP):
        y = conv_taps(lambda a: x[a : a + out_rows], out_rows, width, w_ref, g)
        left = jnp.where(col == 0, 0.0, pltpu.roll(y[0], 1, 0))
        right = jnp.where(col == width - 1, 0.0, pltpu.roll(y[2], n - 1, 0))
        outs.append(y[1] + left + right)
    return jnp.concatenate(outs, axis=-1)


def block_kernel(base_ref, x_ref, win_ref, w1_ref, w2_ref, wout_ref, o_ref):
    rows, width, ch = x_ref.shape
    height = base_ref[1]
    base = base_ref[0]
    x = x_ref[...].astype(jnp.float32).reshape(rows * width, ch)
    pre = (activate(x) * BETA_BLOCK).astype(jnp.bfloat16)
    first = activate(jnp.dot(pre, win_ref[...], preferred_element_type=jnp.float32))
    first = jnp.where(inside_rows(rows, width, base, height), first, 0.0)
    first = first.astype(jnp.bfloat16).astype(jnp.float32).reshape(rows, width, -1)
    second = activate(conv_same(first, w1_ref))
    second = jnp.where(inside_rows(rows - 2, width, base + 1, height), second, 0.0)
    second = second.astype(jnp.bfloat16).astype(jnp.float32).reshape(rows - 2, width, -1)
    third = activate(conv_same(second, w2_ref)).astype(jnp.bfloat16)
    skip = x_ref[2 : rows - 2].astype(jnp.float32).reshape((rows - 4) * width, ch)
    out = skip + RESIDUAL_SCALE * jnp.dot(third, wout_ref[...], preferred_element_type=jnp.float32)
    o_ref[...] = out.astype(o_ref.dtype).reshape(rows - 4, width, ch)


def trans_kernel(base_ref, x_ref, win_ref, w1_ref, w2_ref, wout_ref, wshort_ref, o_ref, pool_scr, sub_scr):
    rows, width, ch = x_ref.shape
    core_rows = rows - 5
    half = width // 2
    height = base_ref[1]
    base = base_ref[0] + 2
    x = x_ref[...].astype(jnp.float32).reshape(rows * width, ch)
    pre = (activate(x) * BETA_TRANSITION).astype(jnp.bfloat16)

    core = pre.astype(jnp.float32).reshape(rows, width, ch)[2 : 2 + core_rows]
    core = core.reshape(core_rows // 2, 2, width, ch)
    summed = (core[:, 0] + core[:, 1]).reshape(core_rows // 2 * width, ch)
    n_pool = core_rows // 2 * half
    parts = []
    for k in range(ch // GROUP):
        pool_scr[k] = summed[:, k * GROUP : (k + 1) * GROUP]
        part = pool_scr.at[k]
        parts.append(part[pl.ds(0, n_pool, stride=2), :] + part[pl.ds(1, n_pool, stride=2), :])
    pooled = (jnp.concatenate(parts, axis=-1) * 0.25).astype(jnp.bfloat16)

    first = activate(jnp.dot(pre, win_ref[...], preferred_element_type=jnp.float32))
    first = jnp.where(inside_rows(rows, width, base, height), first, 0.0)
    first = first.astype(jnp.bfloat16).astype(jnp.float32).reshape(rows, width, -1)
    mid = first.shape[-1]
    first = jnp.concatenate([first, jnp.zeros((1, width, mid), jnp.float32)], axis=0)
    pairs = first.reshape((rows + 1) // 2, 2, width, mid)
    out_rows = (rows - 1) // 2
    picks = (pairs[:out_rows, 0], pairs[:out_rows, 1], pairs[1 : out_rows + 1, 0])
    n = out_rows * width
    col = column_of(out_rows, width)
    for g in range(mid // GROUP):
        y = conv_taps(lambda a: picks[a], out_rows, width, w1_ref, g)
        z = y[0] + pltpu.roll(y[1], n - 1, 0) + jnp.where(col >= width - 2, 0.0, pltpu.roll(y[2], n - 2, 0))
        sub_scr[g, pl.ds(0, n), :] = z
    picked = [sub_scr.at[g][pl.ds(0, out_rows * half, stride=2), :] for g in range(mid // GROUP)]
    second = activate(jnp.concatenate(picked, axis=-1))
    second = jnp.where(inside_rows(out_rows, half, base_ref[0] // 2 + 1, height // 2), second, 0.0)
    second = second.astype(jnp.bfloat16).astype(jnp.float32).reshape(out_rows, half, mid)
    third = activate(conv_same(second, w2_ref)).astype(jnp.bfloat16)
    out = jnp.dot(pooled, wshort_ref[...], preferred_element_type=jnp.float32)
    out = out + RESIDUAL_SCALE * jnp.dot(third, wout_ref[...], preferred_element_type=jnp.float32)
    o_ref[...] = out.astype(o_ref.dtype)


def vmem_call(kernel, out_shape, n_in, scratch=()):
    return pl.pallas_call(
        kernel,
        out_shape=out_shape,
        in_specs=[pl.BlockSpec(memory_space=pltpu.SMEM)] + [pl.BlockSpec(memory_space=pltpu.VMEM)] * n_in,
        out_specs=pl.BlockSpec(memory_space=pltpu.VMEM),
        scratch_shapes=list(scratch),
    )


def compute(strip, base_info, block_in, block_grouped_one, block_grouped_two, block_out,
            trans_in, trans_grouped_one, trans_grouped_two, trans_out, trans_short):
    rows, width, ch = strip.shape
    block_result = vmem_call(block_kernel, jax.ShapeDtypeStruct((rows - 4, width, ch), jnp.bfloat16), 5)(
        base_info, strip, block_in, block_grouped_one, block_grouped_two, block_out
    )
    t_rows = rows - 4
    core_rows = t_rows - 5
    out_rows = (t_rows - 1) // 2
    mid = trans_in.shape[1]
    wide = trans_out.shape[1]
    scratch = (
        pltpu.VMEM((ch // GROUP, core_rows // 2 * width, GROUP), jnp.float32),
        pltpu.VMEM((mid // GROUP, out_rows * width + 8, GROUP), jnp.float32),
    )
    out_shape = jax.ShapeDtypeStruct(((core_rows // 2) * (width // 2), wide), jnp.bfloat16)
    features = vmem_call(trans_kernel, out_shape, 6, scratch)(
        base_info, block_result, trans_in, trans_grouped_one, trans_grouped_two,
        trans_out, trans_short
    )
    return features.reshape(core_rows // 2, width // 2, wide)


def local(
    images,
    block_in,
    block_grouped_one,
    block_grouped_two,
    block_out,
    trans_in,
    trans_grouped_one,
    trans_grouped_two,
    trans_out,
    trans_short,
):
    nrow = lax.axis_size("row")
    ncol = lax.axis_size("col")
    _, n_img, th, tw, ch = images.shape
    c = lax.axis_index("col")
    base_info = jnp.stack([c * th - TOP, th * nrow]).astype(jnp.int32)
    strip = gather_strips(images.reshape(n_img, th, tw, ch), nrow, ncol)
    strip = strip.reshape(TOP + th + BOTTOM, ncol * tw, ch)
    features = compute(strip, base_info, block_in, block_grouped_one, block_grouped_two, block_out,
                       trans_in, trans_grouped_one, trans_grouped_two, trans_out, trans_short)
    return features[None, None]


def solution(mesh):
    in_specs = (P("section", None, "row", "col", None), P(), P(), P(), P(), P(), P(), P(), P(), P())
    out_specs = P("section", "row", "col", None, None)
    return jax.shard_map(local, mesh=mesh, in_specs=in_specs, out_specs=out_specs, check_vma=False)
```

```python
import functools

import jax
import jax.numpy as jnp
from jax import lax
from jax.experimental import pallas as pl
from jax.experimental.pallas import tpu as pltpu
from jax.sharding import PartitionSpec as P

GELU_GAIN = 1.7015
RESIDUAL_SCALE = 0.2
BETA_BLOCK = 0.9805
BETA_TRANSITION = 0.9623
GROUP = 128
MESH = pl.DeviceIdType.MESH

TOP = 4
BOTTOM = 5


def activate(values):
    return GELU_GAIN * jax.nn.gelu(values, approximate=True)


def gather_kernel(nrow, ncol, img_ref, out_ref, send_sem, recv_sem, fwd_send, fwd_recv):
    s = lax.axis_index("section")
    r = lax.axis_index("row")
    c = lax.axis_index("col")
    n_img, th, tw = img_ref.shape[0], img_ref.shape[1], img_ref.shape[2]
    barrier = pltpu.get_barrier_semaphore()

    dests = []
    for i in range(n_img):
        is_self = jnp.logical_and(r == i, r == c)
        dests.append((i, jnp.logical_not(is_self), is_self))
    sources = []
    for cs in range(ncol):
        is_self = jnp.logical_and(c == r, cs == c)
        sources.append((cs, jnp.logical_not(is_self)))
    up = c - 1
    down = c + 1
    has_up = up >= 0
    has_down = down < ncol
    up_id = (s, r, lax.rem(up + ncol, ncol))
    down_id = (s, r, lax.rem(down, ncol))

    for i, is_remote, _ in dests:
        @pl.when(is_remote)
        def _():
            pl.semaphore_signal(barrier, 1, device_id=(s, i, r), device_id_type=MESH)
    for cs, is_remote in sources:
        @pl.when(is_remote)
        def _():
            pl.semaphore_signal(barrier, 1, device_id=(s, c, cs), device_id_type=MESH)
    for flag, dev in ((has_up, up_id), (has_down, down_id)):
        @pl.when(flag)
        def _():
            pl.semaphore_signal(barrier, 1, device_id=dev, device_id_type=MESH)
    peers = [p for _, p, _ in dests] + [p for _, p in sources] + [has_up, has_down]
    pl.semaphore_wait(barrier, sum(p.astype(jnp.int32) for p in peers))

    remote_copies = []
    for k in range(n_img):
        i = lax.rem(c + k, n_img)
        src = img_ref.at[i]
        dst = out_ref.at[pl.ds(TOP, th), c]
        rdesc = pltpu.make_async_remote_copy(
            src_ref=src,
            dst_ref=dst,
            send_sem=send_sem.at[k],
            recv_sem=recv_sem.at[c],
            device_id=(s, i, r),
            device_id_type=MESH,
        )
        is_self = jnp.logical_and(r == c, k == 0)
        is_remote = jnp.logical_not(is_self)

        @pl.when(is_remote)
        def _():
            rdesc.start()

        if k == 0:
            @pl.when(is_self)
            def _():
                pltpu.make_async_copy(src, dst, recv_sem.at[c]).start()

        remote_copies.append((rdesc, is_remote))

    forwards = []
    for k in range(ncol):
        cs = lax.rem(r - k + ncol, ncol)
        dst = out_ref.at[pl.ds(TOP, th), cs]
        pltpu.make_async_copy(dst, dst, recv_sem.at[cs]).wait()
        to_up = pltpu.make_async_remote_copy(
            src_ref=out_ref.at[pl.ds(TOP, BOTTOM), cs],
            dst_ref=out_ref.at[pl.ds(TOP + th, BOTTOM), cs],
            send_sem=fwd_send.at[0, k],
            recv_sem=fwd_recv.at[1, cs],
            device_id=up_id,
            device_id_type=MESH,
        )
        to_down = pltpu.make_async_remote_copy(
            src_ref=out_ref.at[pl.ds(th, TOP), cs],
            dst_ref=out_ref.at[pl.ds(0, TOP), cs],
            send_sem=fwd_send.at[1, k],
            recv_sem=fwd_recv.at[0, cs],
            device_id=down_id,
            device_id_type=MESH,
        )

        @pl.when(has_up)
        def _():
            to_up.start()

        @pl.when(has_down)
        def _():
            to_down.start()

        forwards.append((to_up, to_down, cs))

    for to_up, to_down, cs in forwards:
        @pl.when(has_down)
        def _():
            pltpu.make_async_copy(to_up.dst_ref, to_up.dst_ref, fwd_recv.at[1, cs]).wait()

        @pl.when(has_up)
        def _():
            pltpu.make_async_copy(to_down.dst_ref, to_down.dst_ref, fwd_recv.at[0, cs]).wait()

    for rdesc, is_remote in remote_copies:
        @pl.when(is_remote)
        def _():
            rdesc.wait_send()

    for to_up, to_down, cs in forwards:
        @pl.when(has_up)
        def _():
            to_up.wait_send()

        @pl.when(has_down)
        def _():
            to_down.wait_send()


def gather_strips(tiles, nrow, ncol):
    n_img, th, tw, ch = tiles.shape
    return pl.pallas_call(
        functools.partial(gather_kernel, nrow, ncol),
        out_shape=jax.ShapeDtypeStruct((TOP + th + BOTTOM, ncol, tw, ch), tiles.dtype),
        in_specs=[pl.BlockSpec(memory_space=pl.ANY)],
        out_specs=pl.BlockSpec(memory_space=pl.ANY),
        scratch_shapes=[
            pltpu.SemaphoreType.DMA((n_img,)),
            pltpu.SemaphoreType.DMA((ncol,)),
            pltpu.SemaphoreType.DMA((2, ncol)),
            pltpu.SemaphoreType.DMA((2, ncol)),
        ],
        compiler_params=pltpu.CompilerParams(collective_id=0, has_side_effects=True),
    )(tiles)


def inside_rows(count, width, first, height):
    rows = first + lax.broadcasted_iota(jnp.int32, (count * width, 1), 0) // width
    return jnp.logical_and(rows >= 0, rows < height)


def column_of(count, width):
    return lax.broadcasted_iota(jnp.int32, (count * width, 1), 0) % width


def conv_taps(rows_of, out_rows, width, w_ref, group):
    sl = slice(group * GROUP, (group + 1) * GROUP)
    slab = jnp.concatenate([rows_of(a)[:, :, sl] for a in range(3)], axis=-1)
    slab = slab.reshape(out_rows * width, 3 * GROUP).astype(jnp.bfloat16)
    outs = []
    for b in range(3):
        taps = jnp.concatenate([w_ref[(3 * a + b) * GROUP : (3 * a + b + 1) * GROUP, sl] for a in range(3)], axis=0)
        outs.append(jnp.dot(slab, taps, preferred_element_type=jnp.float32))
    return outs


def conv_same(x, w_ref):
    in_rows, width, channels = x.shape
    out_rows = in_rows - 2
    n = out_rows * width
    col = column_of(out_rows, width)
    outs = []
    for g in range(channels // GROUP):
        y = conv_taps(lambda a: x[a : a + out_rows], out_rows, width, w_ref, g)
        left = jnp.where(col == 0, 0.0, pltpu.roll(y[0], 1, 0))
        right = jnp.where(col == width - 1, 0.0, pltpu.roll(y[2], n - 1, 0))
        outs.append(y[1] + left + right)
    return jnp.concatenate(outs, axis=-1)


def block_kernel(base_ref, x_ref, win_ref, w1_ref, w2_ref, wout_ref, o_ref):
    rows, width, ch = x_ref.shape
    height = base_ref[1]
    base = base_ref[0]
    x = x_ref[...].astype(jnp.float32).reshape(rows * width, ch)
    pre = (activate(x) * BETA_BLOCK).astype(jnp.bfloat16)
    first = activate(jnp.dot(pre, win_ref[...], preferred_element_type=jnp.float32))
    first = jnp.where(inside_rows(rows, width, base, height), first, 0.0)
    first = first.astype(jnp.bfloat16).astype(jnp.float32).reshape(rows, width, -1)
    second = activate(conv_same(first, w1_ref))
    second = jnp.where(inside_rows(rows - 2, width, base + 1, height), second, 0.0)
    second = second.astype(jnp.bfloat16).astype(jnp.float32).reshape(rows - 2, width, -1)
    third = activate(conv_same(second, w2_ref)).astype(jnp.bfloat16)
    skip = x_ref[2 : rows - 2].astype(jnp.float32).reshape((rows - 4) * width, ch)
    out = skip + RESIDUAL_SCALE * jnp.dot(third, wout_ref[...], preferred_element_type=jnp.float32)
    o_ref[...] = out.astype(o_ref.dtype).reshape(rows - 4, width, ch)


def trans_kernel(base_ref, x_ref, win_ref, w1_ref, w2_ref, wout_ref, wshort_ref, o_ref, pool_scr, sub_scr):
    rows, width, ch = x_ref.shape
    core_rows = rows - 5
    half = width // 2
    height = base_ref[1]
    base = base_ref[0] + 2
    x = x_ref[...].astype(jnp.float32).reshape(rows * width, ch)
    pre = (activate(x) * BETA_TRANSITION).astype(jnp.bfloat16)

    core = pre.astype(jnp.float32).reshape(rows, width, ch)[2 : 2 + core_rows]
    core = core.reshape(core_rows // 2, 2, width, ch)
    summed = (core[:, 0] + core[:, 1]).reshape(core_rows // 2 * width, ch)
    n_pool = core_rows // 2 * half
    parts = []
    for k in range(ch // GROUP):
        pool_scr[k] = summed[:, k * GROUP : (k + 1) * GROUP]
        part = pool_scr.at[k]
        parts.append(part[pl.ds(0, n_pool, stride=2), :] + part[pl.ds(1, n_pool, stride=2), :])
    pooled = (jnp.concatenate(parts, axis=-1) * 0.25).astype(jnp.bfloat16)

    first = activate(jnp.dot(pre, win_ref[...], preferred_element_type=jnp.float32))
    first = jnp.where(inside_rows(rows, width, base, height), first, 0.0)
    first = first.astype(jnp.bfloat16).astype(jnp.float32).reshape(rows, width, -1)
    mid = first.shape[-1]
    first = jnp.concatenate([first, jnp.zeros((1, width, mid), jnp.float32)], axis=0)
    pairs = first.reshape((rows + 1) // 2, 2, width, mid)
    out_rows = (rows - 1) // 2
    picks = (pairs[:out_rows, 0], pairs[:out_rows, 1], pairs[1 : out_rows + 1, 0])
    n = out_rows * width
    col = column_of(out_rows, width)
    for g in range(mid // GROUP):
        y = conv_taps(lambda a: picks[a], out_rows, width, w1_ref, g)
        z = y[0] + pltpu.roll(y[1], n - 1, 0) + jnp.where(col >= width - 2, 0.0, pltpu.roll(y[2], n - 2, 0))
        sub_scr[g, pl.ds(0, n), :] = z
    picked = [sub_scr.at[g][pl.ds(0, out_rows * half, stride=2), :] for g in range(mid // GROUP)]
    second = activate(jnp.concatenate(picked, axis=-1))
    second = jnp.where(inside_rows(out_rows, half, base_ref[0] // 2 + 1, height // 2), second, 0.0)
    second = second.astype(jnp.bfloat16).astype(jnp.float32).reshape(out_rows, half, mid)
    third = activate(conv_same(second, w2_ref)).astype(jnp.bfloat16)
    out = jnp.dot(pooled, wshort_ref[...], preferred_element_type=jnp.float32)
    out = out + RESIDUAL_SCALE * jnp.dot(third, wout_ref[...], preferred_element_type=jnp.float32)
    o_ref[...] = out.astype(o_ref.dtype)


def vmem_call(kernel, out_shape, n_in, scratch=()):
    return pl.pallas_call(
        kernel,
        out_shape=out_shape,
        in_specs=[pl.BlockSpec(memory_space=pltpu.SMEM)] + [pl.BlockSpec(memory_space=pltpu.VMEM)] * n_in,
        out_specs=pl.BlockSpec(memory_space=pltpu.VMEM),
        scratch_shapes=list(scratch),
    )


def compute(strip, base_info, block_in, block_grouped_one, block_grouped_two, block_out,
            trans_in, trans_grouped_one, trans_grouped_two, trans_out, trans_short):
    rows, width, ch = strip.shape
    block_result = vmem_call(block_kernel, jax.ShapeDtypeStruct((rows - 4, width, ch), jnp.bfloat16), 5)(
        base_info, strip, block_in, block_grouped_one, block_grouped_two, block_out
    )
    t_rows = rows - 4
    core_rows = t_rows - 5
    out_rows = (t_rows - 1) // 2
    mid = trans_in.shape[1]
    wide = trans_out.shape[1]
    scratch = (
        pltpu.VMEM((ch // GROUP, core_rows // 2 * width, GROUP), jnp.float32),
        pltpu.VMEM((mid // GROUP, out_rows * width + 8, GROUP), jnp.float32),
    )
    out_shape = jax.ShapeDtypeStruct(((core_rows // 2) * (width // 2), wide), jnp.bfloat16)
    features = vmem_call(trans_kernel, out_shape, 6, scratch)(
        base_info, block_result, trans_in, trans_grouped_one, trans_grouped_two,
        trans_out, trans_short
    )
    return features.reshape(core_rows // 2, width // 2, wide)


def local(
    images,
    block_in,
    block_grouped_one,
    block_grouped_two,
    block_out,
    trans_in,
    trans_grouped_one,
    trans_grouped_two,
    trans_out,
    trans_short,
):
    nrow = lax.axis_size("row")
    ncol = lax.axis_size("col")
    _, n_img, th, tw, ch = images.shape
    c = lax.axis_index("col")
    base_info = jnp.stack([c * th - TOP, th * nrow]).astype(jnp.int32)
    strip = gather_strips(images.reshape(n_img, th, tw, ch), nrow, ncol)
    strip = strip.reshape(TOP + th + BOTTOM, ncol * tw, ch)
    features = compute(strip, base_info, block_in, block_grouped_one, block_grouped_two, block_out,
                       trans_in, trans_grouped_one, trans_grouped_two, trans_out, trans_short)
    return features[None, None]


def solution(mesh):
    in_specs = (P("section", None, "row", "col", None), P(), P(), P(), P(), P(), P(), P(), P(), P())
    out_specs = P("section", "row", "col", None, None)
    return jax.shard_map(local, mesh=mesh, in_specs=in_specs, out_specs=out_specs, check_vma=False)
```

```python
import functools

import jax
import jax.numpy as jnp
from jax import lax
from jax.experimental import pallas as pl
from jax.experimental.pallas import tpu as pltpu
from jax.sharding import PartitionSpec as P

GELU_GAIN = 1.7015
RESIDUAL_SCALE = 0.2
BETA_BLOCK = 0.9805
BETA_TRANSITION = 0.9623
GROUP = 128
MESH = pl.DeviceIdType.MESH

TOP = 4
BOTTOM = 5


def activate(values):
    return GELU_GAIN * jax.nn.gelu(values, approximate=True)


def gather_kernel(nrow, ncol, img_ref, out_ref, send_sem, recv_sem, fwd_send, fwd_recv):
    s = lax.axis_index("section")
    r = lax.axis_index("row")
    c = lax.axis_index("col")
    n_img, th, tw = img_ref.shape[0], img_ref.shape[1], img_ref.shape[2]
    barrier = pltpu.get_barrier_semaphore()

    dests = []
    for i in range(n_img):
        is_self = jnp.logical_and(r == i, r == c)
        dests.append((i, jnp.logical_not(is_self), is_self))
    sources = []
    for cs in range(ncol):
        is_self = jnp.logical_and(c == r, cs == c)
        sources.append((cs, jnp.logical_not(is_self)))
    up = c - 1
    down = c + 1
    has_up = up >= 0
    has_down = down < ncol
    up_id = (s, r, lax.rem(up + ncol, ncol))
    down_id = (s, r, lax.rem(down, ncol))

    for i, is_remote, _ in dests:
        @pl.when(is_remote)
        def _():
            pl.semaphore_signal(barrier, 1, device_id=(s, i, r), device_id_type=MESH)
    for cs, is_remote in sources:
        @pl.when(is_remote)
        def _():
            pl.semaphore_signal(barrier, 1, device_id=(s, c, cs), device_id_type=MESH)
    for flag, dev in ((has_up, up_id), (has_down, down_id)):
        @pl.when(flag)
        def _():
            pl.semaphore_signal(barrier, 1, device_id=dev, device_id_type=MESH)
    peers = [p for _, p, _ in dests] + [p for _, p in sources] + [has_up, has_down]
    pl.semaphore_wait(barrier, sum(p.astype(jnp.int32) for p in peers))

    remote_copies = []
    for k in range(n_img):
        i = lax.rem(c + k, n_img)
        src = img_ref.at[i]
        dst = out_ref.at[pl.ds(TOP, th), c]
        rdesc = pltpu.make_async_remote_copy(
            src_ref=src,
            dst_ref=dst,
            send_sem=send_sem.at[k],
            recv_sem=recv_sem.at[c],
            device_id=(s, i, r),
            device_id_type=MESH,
        )
        is_self = jnp.logical_and(r == c, k == 0)
        is_remote = jnp.logical_not(is_self)

        @pl.when(is_remote)
        def _():
            rdesc.start()

        if k == 0:
            @pl.when(is_self)
            def _():
                pltpu.make_async_copy(src, dst, recv_sem.at[c]).start()

        remote_copies.append((rdesc, is_remote))

    forwards = []
    for k in range(ncol):
        cs = lax.rem(r - k + ncol, ncol)
        dst = out_ref.at[pl.ds(TOP, th), cs]
        pltpu.make_async_copy(dst, dst, recv_sem.at[cs]).wait()
        to_up = pltpu.make_async_remote_copy(
            src_ref=out_ref.at[pl.ds(TOP, BOTTOM), cs],
            dst_ref=out_ref.at[pl.ds(TOP + th, BOTTOM), cs],
            send_sem=fwd_send.at[0, k],
            recv_sem=fwd_recv.at[1, cs],
            device_id=up_id,
            device_id_type=MESH,
        )
        to_down = pltpu.make_async_remote_copy(
            src_ref=out_ref.at[pl.ds(th, TOP), cs],
            dst_ref=out_ref.at[pl.ds(0, TOP), cs],
            send_sem=fwd_send.at[1, k],
            recv_sem=fwd_recv.at[0, cs],
            device_id=down_id,
            device_id_type=MESH,
        )

        @pl.when(has_up)
        def _():
            to_up.start()

        @pl.when(has_down)
        def _():
            to_down.start()

        forwards.append((to_up, to_down, cs))

    for to_up, to_down, cs in forwards:
        @pl.when(has_down)
        def _():
            pltpu.make_async_copy(to_up.dst_ref, to_up.dst_ref, fwd_recv.at[1, cs]).wait()

        @pl.when(has_up)
        def _():
            pltpu.make_async_copy(to_down.dst_ref, to_down.dst_ref, fwd_recv.at[0, cs]).wait()

    for rdesc, is_remote in remote_copies:
        @pl.when(is_remote)
        def _():
            rdesc.wait_send()

    for to_up, to_down, cs in forwards:
        @pl.when(has_up)
        def _():
            to_up.wait_send()

        @pl.when(has_down)
        def _():
            to_down.wait_send()


def gather_strips(tiles, nrow, ncol):
    n_img, th, tw, ch = tiles.shape
    return pl.pallas_call(
        functools.partial(gather_kernel, nrow, ncol),
        out_shape=jax.ShapeDtypeStruct((TOP + th + BOTTOM, ncol, tw, ch), tiles.dtype),
        in_specs=[pl.BlockSpec(memory_space=pl.ANY)],
        out_specs=pl.BlockSpec(memory_space=pl.ANY),
        scratch_shapes=[
            pltpu.SemaphoreType.DMA((n_img,)),
            pltpu.SemaphoreType.DMA((ncol,)),
            pltpu.SemaphoreType.DMA((2, ncol)),
            pltpu.SemaphoreType.DMA((2, ncol)),
        ],
        compiler_params=pltpu.CompilerParams(collective_id=0, has_side_effects=True),
    )(tiles)


def inside_rows(count, width, first, height):
    rows = first + lax.broadcasted_iota(jnp.int32, (count * width, 1), 0) // width
    return jnp.logical_and(rows >= 0, rows < height)


def column_of(count, width):
    return lax.broadcasted_iota(jnp.int32, (count * width, 1), 0) % width


def conv_taps(rows_of, out_rows, width, w_ref, group):
    sl = slice(group * GROUP, (group + 1) * GROUP)
    slab = jnp.concatenate([rows_of(a)[:, :, sl] for a in range(3)], axis=-1)
    slab = slab.reshape(out_rows * width, 3 * GROUP).astype(jnp.bfloat16)
    outs = []
    for b in range(3):
        taps = jnp.concatenate([w_ref[(3 * a + b) * GROUP : (3 * a + b + 1) * GROUP, sl] for a in range(3)], axis=0)
        outs.append(jnp.dot(slab, taps, preferred_element_type=jnp.float32))
    return outs


def conv_same(x, w_ref):
    in_rows, width, channels = x.shape
    out_rows = in_rows - 2
    n = out_rows * width
    col = column_of(out_rows, width)
    outs = []
    for g in range(channels // GROUP):
        y = conv_taps(lambda a: x[a : a + out_rows], out_rows, width, w_ref, g)
        left = jnp.where(col == 0, 0.0, pltpu.roll(y[0], 1, 0))
        right = jnp.where(col == width - 1, 0.0, pltpu.roll(y[2], n - 1, 0))
        outs.append(y[1] + left + right)
    return jnp.concatenate(outs, axis=-1)


def block_body(base, height, x, win_ref, w1_ref, w2_ref, wout_ref):
    rows, width, ch = x.shape
    pre = (activate(x.reshape(rows * width, ch)) * BETA_BLOCK).astype(jnp.bfloat16)
    first = activate(jnp.dot(pre, win_ref[...], preferred_element_type=jnp.float32))
    first = jnp.where(inside_rows(rows, width, base, height), first, 0.0)
    first = first.astype(jnp.bfloat16).astype(jnp.float32).reshape(rows, width, -1)
    second = activate(conv_same(first, w1_ref))
    second = jnp.where(inside_rows(rows - 2, width, base + 1, height), second, 0.0)
    second = second.astype(jnp.bfloat16).astype(jnp.float32).reshape(rows - 2, width, -1)
    third = activate(conv_same(second, w2_ref)).astype(jnp.bfloat16)
    skip = x[2 : rows - 2].reshape((rows - 4) * width, ch)
    out = skip + RESIDUAL_SCALE * jnp.dot(third, wout_ref[...], preferred_element_type=jnp.float32)
    return out.astype(jnp.bfloat16)


def fused_kernel(base_ref, x_ref, bin_ref, b1_ref, b2_ref, bout_ref,
                 win_ref, w1_ref, w2_ref, wout_ref, wshort_ref, o_ref, pool_scr, sub_scr):
    in_rows, blocks, block_width, ch = x_ref.shape
    strip = jnp.concatenate([x_ref[:, cb].astype(jnp.float32) for cb in range(blocks)], axis=1)
    height = base_ref[1]
    block_result = block_body(base_ref[0], height, strip, bin_ref, b1_ref, b2_ref, bout_ref)
    rows = in_rows - 4
    width = blocks * block_width
    core_rows = rows - 5
    half = width // 2
    base = base_ref[0] + 2
    x = block_result.astype(jnp.float32)
    pre = (activate(x) * BETA_TRANSITION).astype(jnp.bfloat16)

    core = pre.astype(jnp.float32).reshape(rows, width, ch)[2 : 2 + core_rows]
    core = core.reshape(core_rows // 2, 2, width, ch)
    summed = (core[:, 0] + core[:, 1]).reshape(core_rows // 2 * width, ch)
    n_pool = core_rows // 2 * half
    parts = []
    for k in range(ch // GROUP):
        pool_scr[k] = summed[:, k * GROUP : (k + 1) * GROUP]
        part = pool_scr.at[k]
        parts.append(part[pl.ds(0, n_pool, stride=2), :] + part[pl.ds(1, n_pool, stride=2), :])
    pooled = (jnp.concatenate(parts, axis=-1) * 0.25).astype(jnp.bfloat16)

    first = activate(jnp.dot(pre, win_ref[...], preferred_element_type=jnp.float32))
    first = jnp.where(inside_rows(rows, width, base, height), first, 0.0)
    first = first.astype(jnp.bfloat16).astype(jnp.float32).reshape(rows, width, -1)
    mid = first.shape[-1]
    first = jnp.concatenate([first, jnp.zeros((1, width, mid), jnp.float32)], axis=0)
    pairs = first.reshape((rows + 1) // 2, 2, width, mid)
    out_rows = (rows - 1) // 2
    picks = (pairs[:out_rows, 0], pairs[:out_rows, 1], pairs[1 : out_rows + 1, 0])
    n = out_rows * width
    col = column_of(out_rows, width)
    for g in range(mid // GROUP):
        y = conv_taps(lambda a: picks[a], out_rows, width, w1_ref, g)
        z = y[0] + pltpu.roll(y[1], n - 1, 0) + jnp.where(col >= width - 2, 0.0, pltpu.roll(y[2], n - 2, 0))
        sub_scr[g, pl.ds(0, n), :] = z
    picked = [sub_scr.at[g][pl.ds(0, out_rows * half, stride=2), :] for g in range(mid // GROUP)]
    second = activate(jnp.concatenate(picked, axis=-1))
    second = jnp.where(inside_rows(out_rows, half, base_ref[0] // 2 + 1, height // 2), second, 0.0)
    second = second.astype(jnp.bfloat16).astype(jnp.float32).reshape(out_rows, half, mid)
    third = activate(conv_same(second, w2_ref)).astype(jnp.bfloat16)
    out = jnp.dot(pooled, wshort_ref[...], preferred_element_type=jnp.float32)
    out = out + RESIDUAL_SCALE * jnp.dot(third, wout_ref[...], preferred_element_type=jnp.float32)
    o_ref[...] = out.astype(o_ref.dtype)


def vmem_call(kernel, out_shape, n_in, scratch=()):
    return pl.pallas_call(
        kernel,
        out_shape=out_shape,
        in_specs=[pl.BlockSpec(memory_space=pltpu.SMEM)] + [pl.BlockSpec(memory_space=pltpu.VMEM)] * n_in,
        out_specs=pl.BlockSpec(memory_space=pltpu.VMEM),
        scratch_shapes=list(scratch),
    )


def compute(strip, base_info, block_in, block_grouped_one, block_grouped_two, block_out,
            trans_in, trans_grouped_one, trans_grouped_two, trans_out, trans_short):
    in_rows, blocks, block_width, ch = strip.shape
    width = blocks * block_width
    t_rows = in_rows - 4
    core_rows = t_rows - 5
    out_rows = (t_rows - 1) // 2
    mid = trans_in.shape[1]
    wide = trans_out.shape[1]
    scratch = (
        pltpu.VMEM((ch // GROUP, core_rows // 2 * width, GROUP), jnp.float32),
        pltpu.VMEM((mid // GROUP, out_rows * width + 8, GROUP), jnp.float32),
    )
    out_shape = jax.ShapeDtypeStruct(((core_rows // 2) * (width // 2), wide), jnp.bfloat16)
    features = vmem_call(fused_kernel, out_shape, 10, scratch)(
        base_info, strip, block_in, block_grouped_one, block_grouped_two, block_out,
        trans_in, trans_grouped_one, trans_grouped_two, trans_out, trans_short
    )
    return features.reshape(core_rows // 2, width // 2, wide)


def local(
    images,
    block_in,
    block_grouped_one,
    block_grouped_two,
    block_out,
    trans_in,
    trans_grouped_one,
    trans_grouped_two,
    trans_out,
    trans_short,
):
    nrow = lax.axis_size("row")
    ncol = lax.axis_size("col")
    _, n_img, th, tw, ch = images.shape
    c = lax.axis_index("col")
    base_info = jnp.stack([c * th - TOP, th * nrow]).astype(jnp.int32)
    strip = gather_strips(images.reshape(n_img, th, tw, ch), nrow, ncol)
    features = compute(strip, base_info, block_in, block_grouped_one, block_grouped_two, block_out,
                       trans_in, trans_grouped_one, trans_grouped_two, trans_out, trans_short)
    return features[None, None]


def solution(mesh):
    in_specs = (P("section", None, "row", "col", None), P(), P(), P(), P(), P(), P(), P(), P(), P())
    out_specs = P("section", "row", "col", None, None)
    return jax.shard_map(local, mesh=mesh, in_specs=in_specs, out_specs=out_specs, check_vma=False)
```

```python
import functools

import jax
import jax.numpy as jnp
from jax import lax
from jax.experimental import pallas as pl
from jax.experimental.pallas import tpu as pltpu
from jax.sharding import PartitionSpec as P

GELU_GAIN = 1.7015
RESIDUAL_SCALE = 0.2
BETA_BLOCK = 0.9805
BETA_TRANSITION = 0.9623
GROUP = 128
MESH = pl.DeviceIdType.MESH

TOP = 4
BOTTOM = 5


def activate(values):
    return GELU_GAIN * jax.nn.gelu(values, approximate=True)


def gather_kernel(nrow, ncol, img_ref, out_ref, send_sem, recv_sem, fwd_send, fwd_recv):
    s = lax.axis_index("section")
    r = lax.axis_index("row")
    c = lax.axis_index("col")
    n_img, th, tw = img_ref.shape[0], img_ref.shape[1], img_ref.shape[2]
    barrier = pltpu.get_barrier_semaphore()

    dests = []
    for i in range(n_img):
        is_self = jnp.logical_and(r == i, r == c)
        dests.append((i, jnp.logical_not(is_self), is_self))
    sources = []
    for cs in range(ncol):
        is_self = jnp.logical_and(c == r, cs == c)
        sources.append((cs, jnp.logical_not(is_self)))
    up = c - 1
    down = c + 1
    has_up = up >= 0
    has_down = down < ncol
    up_id = (s, r, lax.rem(up + ncol, ncol))
    down_id = (s, r, lax.rem(down, ncol))

    for i, is_remote, _ in dests:
        @pl.when(is_remote)
        def _():
            pl.semaphore_signal(barrier, 1, device_id=(s, i, r), device_id_type=MESH)
    for cs, is_remote in sources:
        @pl.when(is_remote)
        def _():
            pl.semaphore_signal(barrier, 1, device_id=(s, c, cs), device_id_type=MESH)
    for flag, dev in ((has_up, up_id), (has_down, down_id)):
        @pl.when(flag)
        def _():
            pl.semaphore_signal(barrier, 1, device_id=dev, device_id_type=MESH)
    peers = [p for _, p, _ in dests] + [p for _, p in sources] + [has_up, has_down]
    pl.semaphore_wait(barrier, sum(p.astype(jnp.int32) for p in peers))

    remote_copies = []
    for k in range(n_img):
        i = lax.rem(c + k, n_img)
        src = img_ref.at[i]
        dst = out_ref.at[pl.ds(TOP, th), c]
        rdesc = pltpu.make_async_remote_copy(
            src_ref=src,
            dst_ref=dst,
            send_sem=send_sem.at[k],
            recv_sem=recv_sem.at[c],
            device_id=(s, i, r),
            device_id_type=MESH,
        )
        is_self = jnp.logical_and(r == c, k == 0)
        is_remote = jnp.logical_not(is_self)

        @pl.when(is_remote)
        def _():
            rdesc.start()

        if k == 0:
            @pl.when(is_self)
            def _():
                pltpu.make_async_copy(src, dst, recv_sem.at[c]).start()

        remote_copies.append((rdesc, is_remote))

    forwards = []
    for k in range(ncol):
        cs = lax.rem(r - k + ncol, ncol)
        dst = out_ref.at[pl.ds(TOP, th), cs]
        pltpu.make_async_copy(dst, dst, recv_sem.at[cs]).wait()
        to_up = pltpu.make_async_remote_copy(
            src_ref=out_ref.at[pl.ds(TOP, BOTTOM), cs],
            dst_ref=out_ref.at[pl.ds(TOP + th, BOTTOM), cs],
            send_sem=fwd_send.at[0, k],
            recv_sem=fwd_recv.at[1, cs],
            device_id=up_id,
            device_id_type=MESH,
        )
        to_down = pltpu.make_async_remote_copy(
            src_ref=out_ref.at[pl.ds(th, TOP), cs],
            dst_ref=out_ref.at[pl.ds(0, TOP), cs],
            send_sem=fwd_send.at[1, k],
            recv_sem=fwd_recv.at[0, cs],
            device_id=down_id,
            device_id_type=MESH,
        )

        @pl.when(has_up)
        def _():
            to_up.start()

        @pl.when(has_down)
        def _():
            to_down.start()

        forwards.append((to_up, to_down, cs))

    for to_up, to_down, cs in forwards:
        @pl.when(has_down)
        def _():
            pltpu.make_async_copy(to_up.dst_ref, to_up.dst_ref, fwd_recv.at[1, cs]).wait()

        @pl.when(has_up)
        def _():
            pltpu.make_async_copy(to_down.dst_ref, to_down.dst_ref, fwd_recv.at[0, cs]).wait()

    for rdesc, is_remote in remote_copies:
        @pl.when(is_remote)
        def _():
            rdesc.wait_send()

    for to_up, to_down, cs in forwards:
        @pl.when(has_up)
        def _():
            to_up.wait_send()

        @pl.when(has_down)
        def _():
            to_down.wait_send()


def gather_strips(tiles, nrow, ncol):
    n_img, th, tw, ch = tiles.shape
    return pl.pallas_call(
        functools.partial(gather_kernel, nrow, ncol),
        out_shape=jax.ShapeDtypeStruct((TOP + th + BOTTOM, ncol, tw, ch), tiles.dtype),
        in_specs=[pl.BlockSpec(memory_space=pl.ANY)],
        out_specs=pl.BlockSpec(memory_space=pl.ANY),
        scratch_shapes=[
            pltpu.SemaphoreType.DMA((n_img,)),
            pltpu.SemaphoreType.DMA((ncol,)),
            pltpu.SemaphoreType.DMA((2, ncol)),
            pltpu.SemaphoreType.DMA((2, ncol)),
        ],
        compiler_params=pltpu.CompilerParams(collective_id=0, has_side_effects=True),
    )(tiles)


def inside_rows(count, width, first, height):
    rows = first + lax.broadcasted_iota(jnp.int32, (count * width, 1), 0) // width
    return jnp.logical_and(rows >= 0, rows < height)


def column_of(count, width):
    return lax.broadcasted_iota(jnp.int32, (count * width, 1), 0) % width


def conv_taps(rows_of, out_rows, width, w_ref, group):
    sl = slice(group * GROUP, (group + 1) * GROUP)
    slab = jnp.concatenate([rows_of(a)[:, :, sl] for a in range(3)], axis=-1)
    slab = slab.reshape(out_rows * width, 3 * GROUP).astype(jnp.bfloat16)
    outs = []
    for b in range(3):
        taps = jnp.concatenate([w_ref[(3 * a + b) * GROUP : (3 * a + b + 1) * GROUP, sl] for a in range(3)], axis=0)
        outs.append(jnp.dot(slab, taps, preferred_element_type=jnp.float32))
    return outs


def conv_same(x, w_ref):
    in_rows, width, channels = x.shape
    out_rows = in_rows - 2
    n = out_rows * width
    col = column_of(out_rows, width)
    outs = []
    for g in range(channels // GROUP):
        y = conv_taps(lambda a: x[a : a + out_rows], out_rows, width, w_ref, g)
        left = jnp.where(col == 0, 0.0, pltpu.roll(y[0], 1, 0))
        right = jnp.where(col == width - 1, 0.0, pltpu.roll(y[2], n - 1, 0))
        outs.append(y[1] + left + right)
    return jnp.concatenate(outs, axis=-1)


def block_body(base, height, x, win_ref, w1_ref, w2_ref, wout_ref):
    rows, width, ch = x.shape
    pre = (activate(x.reshape(rows * width, ch)) * BETA_BLOCK).astype(jnp.bfloat16)
    first = activate(jnp.dot(pre, win_ref[...], preferred_element_type=jnp.float32))
    first = jnp.where(inside_rows(rows, width, base, height), first, 0.0)
    first = first.astype(jnp.bfloat16).astype(jnp.float32).reshape(rows, width, -1)
    second = activate(conv_same(first, w1_ref))
    second = jnp.where(inside_rows(rows - 2, width, base + 1, height), second, 0.0)
    second = second.astype(jnp.bfloat16).astype(jnp.float32).reshape(rows - 2, width, -1)
    third = activate(conv_same(second, w2_ref)).astype(jnp.bfloat16)
    skip = x[2 : rows - 2].reshape((rows - 4) * width, ch)
    out = skip + RESIDUAL_SCALE * jnp.dot(third, wout_ref[...], preferred_element_type=jnp.float32)
    return out.astype(jnp.bfloat16)


def fused_kernel(base_ref, x_ref, bin_ref, b1_ref, b2_ref, bout_ref,
                 win_ref, w1_ref, w2_ref, wout_ref, wshort_ref, o_ref, pool_scr, sub_scr):
    in_rows, width, ch = x_ref.shape
    strip = x_ref[...].astype(jnp.float32)
    height = base_ref[1]
    block_result = block_body(base_ref[0], height, strip, bin_ref, b1_ref, b2_ref, bout_ref)
    rows = in_rows - 4
    core_rows = rows - 5
    half = width // 2
    base = base_ref[0] + 2
    x = block_result.astype(jnp.float32)
    pre = (activate(x) * BETA_TRANSITION).astype(jnp.bfloat16)

    core = pre.astype(jnp.float32).reshape(rows, width, ch)[2 : 2 + core_rows]
    core = core.reshape(core_rows // 2, 2, width, ch)
    summed = (core[:, 0] + core[:, 1]).reshape(core_rows // 2 * width, ch)
    n_pool = core_rows // 2 * half
    parts = []
    for k in range(ch // GROUP):
        pool_scr[k] = summed[:, k * GROUP : (k + 1) * GROUP]
        part = pool_scr.at[k]
        parts.append(part[pl.ds(0, n_pool, stride=2), :] + part[pl.ds(1, n_pool, stride=2), :])
    pooled = (jnp.concatenate(parts, axis=-1) * 0.25).astype(jnp.bfloat16)

    first = activate(jnp.dot(pre, win_ref[...], preferred_element_type=jnp.float32))
    first = jnp.where(inside_rows(rows, width, base, height), first, 0.0)
    first = first.astype(jnp.bfloat16).astype(jnp.float32).reshape(rows, width, -1)
    mid = first.shape[-1]
    first = jnp.concatenate([first, jnp.zeros((1, width, mid), jnp.float32)], axis=0)
    pairs = first.reshape((rows + 1) // 2, 2, width, mid)
    out_rows = (rows - 1) // 2
    picks = (pairs[:out_rows, 0], pairs[:out_rows, 1], pairs[1 : out_rows + 1, 0])
    n = out_rows * width
    col = column_of(out_rows, width)
    for g in range(mid // GROUP):
        y = conv_taps(lambda a: picks[a], out_rows, width, w1_ref, g)
        z = y[0] + pltpu.roll(y[1], n - 1, 0) + jnp.where(col >= width - 2, 0.0, pltpu.roll(y[2], n - 2, 0))
        sub_scr[g, pl.ds(0, n), :] = z
    picked = [sub_scr.at[g][pl.ds(0, out_rows * half, stride=2), :] for g in range(mid // GROUP)]
    second = activate(jnp.concatenate(picked, axis=-1))
    second = jnp.where(inside_rows(out_rows, half, base_ref[0] // 2 + 1, height // 2), second, 0.0)
    second = second.astype(jnp.bfloat16).astype(jnp.float32).reshape(out_rows, half, mid)
    third = activate(conv_same(second, w2_ref)).astype(jnp.bfloat16)
    out = jnp.dot(pooled, wshort_ref[...], preferred_element_type=jnp.float32)
    out = out + RESIDUAL_SCALE * jnp.dot(third, wout_ref[...], preferred_element_type=jnp.float32)
    o_ref[...] = out.astype(o_ref.dtype)


def vmem_call(kernel, out_shape, n_in, scratch=()):
    return pl.pallas_call(
        kernel,
        out_shape=out_shape,
        in_specs=[pl.BlockSpec(memory_space=pltpu.SMEM)] + [pl.BlockSpec(memory_space=pltpu.VMEM)] * n_in,
        out_specs=pl.BlockSpec(memory_space=pltpu.VMEM),
        scratch_shapes=list(scratch),
    )


def compute(strip, base_info, block_in, block_grouped_one, block_grouped_two, block_out,
            trans_in, trans_grouped_one, trans_grouped_two, trans_out, trans_short):
    in_rows, width, ch = strip.shape
    t_rows = in_rows - 4
    core_rows = t_rows - 5
    out_rows = (t_rows - 1) // 2
    mid = trans_in.shape[1]
    wide = trans_out.shape[1]
    scratch = (
        pltpu.VMEM((ch // GROUP, core_rows // 2 * width, GROUP), jnp.float32),
        pltpu.VMEM((mid // GROUP, out_rows * width + 8, GROUP), jnp.float32),
    )
    out_shape = jax.ShapeDtypeStruct(((core_rows // 2) * (width // 2), wide), jnp.bfloat16)
    features = vmem_call(fused_kernel, out_shape, 10, scratch)(
        base_info, strip, block_in, block_grouped_one, block_grouped_two, block_out,
        trans_in, trans_grouped_one, trans_grouped_two, trans_out, trans_short
    )
    return features.reshape(core_rows // 2, width // 2, wide)


def local(
    images,
    block_in,
    block_grouped_one,
    block_grouped_two,
    block_out,
    trans_in,
    trans_grouped_one,
    trans_grouped_two,
    trans_out,
    trans_short,
):
    nrow = lax.axis_size("row")
    ncol = lax.axis_size("col")
    _, n_img, th, tw, ch = images.shape
    c = lax.axis_index("col")
    base_info = jnp.stack([c * th - TOP, th * nrow]).astype(jnp.int32)
    tiles = images.reshape(n_img, th, tw * (ch // GROUP), GROUP)
    strip = gather_strips(tiles, nrow, ncol).reshape(TOP + th + BOTTOM, ncol * tw, ch)
    features = compute(strip, base_info, block_in, block_grouped_one, block_grouped_two, block_out,
                       trans_in, trans_grouped_one, trans_grouped_two, trans_out, trans_short)
    return features[None, None]


def solution(mesh):
    in_specs = (P("section", None, "row", "col", None), P(), P(), P(), P(), P(), P(), P(), P(), P())
    out_specs = P("section", "row", "col", None, None)
    return jax.shard_map(local, mesh=mesh, in_specs=in_specs, out_specs=out_specs, check_vma=False)
```

```python
import functools

import jax
import jax.numpy as jnp
from jax import lax
from jax.experimental import pallas as pl
from jax.experimental.pallas import tpu as pltpu
from jax.sharding import PartitionSpec as P

GELU_GAIN = 1.7015
RESIDUAL_SCALE = 0.2
BETA_BLOCK = 0.9805
BETA_TRANSITION = 0.9623
GROUP = 128
MESH = pl.DeviceIdType.MESH

TOP = 4
BOTTOM = 5


def activate(values):
    return GELU_GAIN * jax.nn.gelu(values, approximate=True)


def gather_kernel(nrow, ncol, th, unit, img_ref, out_ref, send_sem, recv_sem, fwd_send, fwd_recv):
    s = lax.axis_index("section")
    r = lax.axis_index("row")
    c = lax.axis_index("col")
    n_img = img_ref.shape[0]
    barrier = pltpu.get_barrier_semaphore()

    dests = []
    for i in range(n_img):
        is_self = jnp.logical_and(r == i, r == c)
        dests.append((i, jnp.logical_not(is_self), is_self))
    sources = []
    for cs in range(ncol):
        is_self = jnp.logical_and(c == r, cs == c)
        sources.append((cs, jnp.logical_not(is_self)))
    up = c - 1
    down = c + 1
    has_up = up >= 0
    has_down = down < ncol
    up_id = (s, r, lax.rem(up + ncol, ncol))
    down_id = (s, r, lax.rem(down, ncol))

    for i, is_remote, _ in dests:
        @pl.when(is_remote)
        def _():
            pl.semaphore_signal(barrier, 1, device_id=(s, i, r), device_id_type=MESH)
    for cs, is_remote in sources:
        @pl.when(is_remote)
        def _():
            pl.semaphore_signal(barrier, 1, device_id=(s, c, cs), device_id_type=MESH)
    for flag, dev in ((has_up, up_id), (has_down, down_id)):
        @pl.when(flag)
        def _():
            pl.semaphore_signal(barrier, 1, device_id=dev, device_id_type=MESH)
    peers = [p for _, p, _ in dests] + [p for _, p in sources] + [has_up, has_down]
    pl.semaphore_wait(barrier, sum(p.astype(jnp.int32) for p in peers))

    remote_copies = []
    for k in range(n_img):
        i = lax.rem(c + k, n_img)
        src = img_ref.at[i]
        dst = out_ref.at[c, pl.ds(TOP * unit, th * unit)]
        rdesc = pltpu.make_async_remote_copy(
            src_ref=src,
            dst_ref=dst,
            send_sem=send_sem.at[k],
            recv_sem=recv_sem.at[c],
            device_id=(s, i, r),
            device_id_type=MESH,
        )
        is_self = jnp.logical_and(r == c, k == 0)
        is_remote = jnp.logical_not(is_self)

        @pl.when(is_remote)
        def _():
            rdesc.start()

        if k == 0:
            @pl.when(is_self)
            def _():
                pltpu.make_async_copy(src, dst, recv_sem.at[c]).start()

        remote_copies.append((rdesc, is_remote))

    forwards = []
    for k in range(ncol):
        cs = lax.rem(r - k + ncol, ncol)
        dst = out_ref.at[cs, pl.ds(TOP * unit, th * unit)]
        pltpu.make_async_copy(dst, dst, recv_sem.at[cs]).wait()
        to_up = pltpu.make_async_remote_copy(
            src_ref=out_ref.at[cs, pl.ds(TOP * unit, BOTTOM * unit)],
            dst_ref=out_ref.at[cs, pl.ds((TOP + th) * unit, BOTTOM * unit)],
            send_sem=fwd_send.at[0, k],
            recv_sem=fwd_recv.at[1, cs],
            device_id=up_id,
            device_id_type=MESH,
        )
        to_down = pltpu.make_async_remote_copy(
            src_ref=out_ref.at[cs, pl.ds(th * unit, TOP * unit)],
            dst_ref=out_ref.at[cs, pl.ds(0, TOP * unit)],
            send_sem=fwd_send.at[1, k],
            recv_sem=fwd_recv.at[0, cs],
            device_id=down_id,
            device_id_type=MESH,
        )

        @pl.when(has_up)
        def _():
            to_up.start()

        @pl.when(has_down)
        def _():
            to_down.start()

        forwards.append((to_up, to_down, cs))

    for to_up, to_down, cs in forwards:
        @pl.when(has_down)
        def _():
            pltpu.make_async_copy(to_up.dst_ref, to_up.dst_ref, fwd_recv.at[1, cs]).wait()

        @pl.when(has_up)
        def _():
            pltpu.make_async_copy(to_down.dst_ref, to_down.dst_ref, fwd_recv.at[0, cs]).wait()

    for rdesc, is_remote in remote_copies:
        @pl.when(is_remote)
        def _():
            rdesc.wait_send()

    for to_up, to_down, cs in forwards:
        @pl.when(has_up)
        def _():
            to_up.wait_send()

        @pl.when(has_down)
        def _():
            to_down.wait_send()


def gather_strips(tiles, nrow, ncol, th):
    n_img, flat, lanes = tiles.shape
    unit = flat // th
    return pl.pallas_call(
        functools.partial(gather_kernel, nrow, ncol, th, unit),
        out_shape=jax.ShapeDtypeStruct((ncol, (TOP + th + BOTTOM) * unit, lanes), tiles.dtype),
        in_specs=[pl.BlockSpec(memory_space=pl.ANY)],
        out_specs=pl.BlockSpec(memory_space=pl.ANY),
        scratch_shapes=[
            pltpu.SemaphoreType.DMA((n_img,)),
            pltpu.SemaphoreType.DMA((ncol,)),
            pltpu.SemaphoreType.DMA((2, ncol)),
            pltpu.SemaphoreType.DMA((2, ncol)),
        ],
        compiler_params=pltpu.CompilerParams(collective_id=0, has_side_effects=True),
    )(tiles)


def inside_rows(count, width, first, height):
    rows = first + lax.broadcasted_iota(jnp.int32, (count * width, 1), 0) // width
    return jnp.logical_and(rows >= 0, rows < height)


def column_of(count, width):
    return lax.broadcasted_iota(jnp.int32, (count * width, 1), 0) % width


def conv_taps(rows_of, out_rows, width, w_ref, group):
    sl = slice(group * GROUP, (group + 1) * GROUP)
    slab = jnp.concatenate([rows_of(a)[:, :, sl] for a in range(3)], axis=-1)
    slab = slab.reshape(out_rows * width, 3 * GROUP).astype(jnp.bfloat16)
    outs = []
    for b in range(3):
        taps = jnp.concatenate([w_ref[(3 * a + b) * GROUP : (3 * a + b + 1) * GROUP, sl] for a in range(3)], axis=0)
        outs.append(jnp.dot(slab, taps, preferred_element_type=jnp.float32))
    return outs


def conv_same(x, w_ref):
    in_rows, width, channels = x.shape
    out_rows = in_rows - 2
    n = out_rows * width
    col = column_of(out_rows, width)
    outs = []
    for g in range(channels // GROUP):
        y = conv_taps(lambda a: x[a : a + out_rows], out_rows, width, w_ref, g)
        left = jnp.where(col == 0, 0.0, pltpu.roll(y[0], 1, 0))
        right = jnp.where(col == width - 1, 0.0, pltpu.roll(y[2], n - 1, 0))
        outs.append(y[1] + left + right)
    return jnp.concatenate(outs, axis=-1)


def block_body(base, height, x, win_ref, w1_ref, w2_ref, wout_ref):
    rows, width, ch = x.shape
    pre = (activate(x.reshape(rows * width, ch)) * BETA_BLOCK).astype(jnp.bfloat16)
    first = activate(jnp.dot(pre, win_ref[...], preferred_element_type=jnp.float32))
    first = jnp.where(inside_rows(rows, width, base, height), first, 0.0)
    first = first.astype(jnp.bfloat16).astype(jnp.float32).reshape(rows, width, -1)
    second = activate(conv_same(first, w1_ref))
    second = jnp.where(inside_rows(rows - 2, width, base + 1, height), second, 0.0)
    second = second.astype(jnp.bfloat16).astype(jnp.float32).reshape(rows - 2, width, -1)
    third = activate(conv_same(second, w2_ref)).astype(jnp.bfloat16)
    skip = x[2 : rows - 2].reshape((rows - 4) * width, ch)
    out = skip + RESIDUAL_SCALE * jnp.dot(third, wout_ref[...], preferred_element_type=jnp.float32)
    return out.astype(jnp.bfloat16)


def fused_kernel(base_ref, x_ref, bin_ref, b1_ref, b2_ref, bout_ref,
                 win_ref, w1_ref, w2_ref, wout_ref, wshort_ref, o_ref, pool_scr, sub_scr):
    in_rows, width, ch = x_ref.shape
    strip = x_ref[...].astype(jnp.float32)
    height = base_ref[1]
    block_result = block_body(base_ref[0], height, strip, bin_ref, b1_ref, b2_ref, bout_ref)
    rows = in_rows - 4
    core_rows = rows - 5
    half = width // 2
    base = base_ref[0] + 2
    x = block_result.astype(jnp.float32)
    pre = (activate(x) * BETA_TRANSITION).astype(jnp.bfloat16)

    core = pre.astype(jnp.float32).reshape(rows, width, ch)[2 : 2 + core_rows]
    core = core.reshape(core_rows // 2, 2, width, ch)
    summed = (core[:, 0] + core[:, 1]).reshape(core_rows // 2 * width, ch)
    n_pool = core_rows // 2 * half
    parts = []
    for k in range(ch // GROUP):
        pool_scr[k] = summed[:, k * GROUP : (k + 1) * GROUP]
        part = pool_scr.at[k]
        parts.append(part[pl.ds(0, n_pool, stride=2), :] + part[pl.ds(1, n_pool, stride=2), :])
    pooled = (jnp.concatenate(parts, axis=-1) * 0.25).astype(jnp.bfloat16)

    first = activate(jnp.dot(pre, win_ref[...], preferred_element_type=jnp.float32))
    first = jnp.where(inside_rows(rows, width, base, height), first, 0.0)
    first = first.astype(jnp.bfloat16).astype(jnp.float32).reshape(rows, width, -1)
    mid = first.shape[-1]
    first = jnp.concatenate([first, jnp.zeros((1, width, mid), jnp.float32)], axis=0)
    pairs = first.reshape((rows + 1) // 2, 2, width, mid)
    out_rows = (rows - 1) // 2
    picks = (pairs[:out_rows, 0], pairs[:out_rows, 1], pairs[1 : out_rows + 1, 0])
    n = out_rows * width
    col = column_of(out_rows, width)
    for g in range(mid // GROUP):
        y = conv_taps(lambda a: picks[a], out_rows, width, w1_ref, g)
        z = y[0] + pltpu.roll(y[1], n - 1, 0) + jnp.where(col >= width - 2, 0.0, pltpu.roll(y[2], n - 2, 0))
        sub_scr[g, pl.ds(0, n), :] = z
    picked = [sub_scr.at[g][pl.ds(0, out_rows * half, stride=2), :] for g in range(mid // GROUP)]
    second = activate(jnp.concatenate(picked, axis=-1))
    second = jnp.where(inside_rows(out_rows, half, base_ref[0] // 2 + 1, height // 2), second, 0.0)
    second = second.astype(jnp.bfloat16).astype(jnp.float32).reshape(out_rows, half, mid)
    third = activate(conv_same(second, w2_ref)).astype(jnp.bfloat16)
    out = jnp.dot(pooled, wshort_ref[...], preferred_element_type=jnp.float32)
    out = out + RESIDUAL_SCALE * jnp.dot(third, wout_ref[...], preferred_element_type=jnp.float32)
    o_ref[...] = out.astype(o_ref.dtype)


def vmem_call(kernel, out_shape, n_in, scratch=()):
    return pl.pallas_call(
        kernel,
        out_shape=out_shape,
        in_specs=[pl.BlockSpec(memory_space=pltpu.SMEM)] + [pl.BlockSpec(memory_space=pltpu.VMEM)] * n_in,
        out_specs=pl.BlockSpec(memory_space=pltpu.VMEM),
        scratch_shapes=list(scratch),
    )


def compute(strip, base_info, block_in, block_grouped_one, block_grouped_two, block_out,
            trans_in, trans_grouped_one, trans_grouped_two, trans_out, trans_short):
    in_rows, width, ch = strip.shape
    t_rows = in_rows - 4
    core_rows = t_rows - 5
    out_rows = (t_rows - 1) // 2
    mid = trans_in.shape[1]
    wide = trans_out.shape[1]
    scratch = (
        pltpu.VMEM((ch // GROUP, core_rows // 2 * width, GROUP), jnp.float32),
        pltpu.VMEM((mid // GROUP, out_rows * width + 8, GROUP), jnp.float32),
    )
    out_shape = jax.ShapeDtypeStruct(((core_rows // 2) * (width // 2), wide), jnp.bfloat16)
    features = vmem_call(fused_kernel, out_shape, 10, scratch)(
        base_info, strip, block_in, block_grouped_one, block_grouped_two, block_out,
        trans_in, trans_grouped_one, trans_grouped_two, trans_out, trans_short
    )
    return features.reshape(core_rows // 2, width // 2, wide)


def local(
    images,
    block_in,
    block_grouped_one,
    block_grouped_two,
    block_out,
    trans_in,
    trans_grouped_one,
    trans_grouped_two,
    trans_out,
    trans_short,
):
    nrow = lax.axis_size("row")
    ncol = lax.axis_size("col")
    _, n_img, th, tw, ch = images.shape
    c = lax.axis_index("col")
    base_info = jnp.stack([c * th - TOP, th * nrow]).astype(jnp.int32)
    tiles = images.reshape(n_img, th * tw * (ch // GROUP), GROUP)
    strip = gather_strips(tiles, nrow, ncol, th).reshape(ncol, TOP + th + BOTTOM, tw, ch)
    strip = strip.transpose(1, 0, 2, 3).reshape(TOP + th + BOTTOM, ncol * tw, ch)
    features = compute(strip, base_info, block_in, block_grouped_one, block_grouped_two, block_out,
                       trans_in, trans_grouped_one, trans_grouped_two, trans_out, trans_short)
    return features[None, None]


def solution(mesh):
    in_specs = (P("section", None, "row", "col", None), P(), P(), P(), P(), P(), P(), P(), P(), P())
    out_specs = P("section", "row", "col", None, None)
    return jax.shard_map(local, mesh=mesh, in_specs=in_specs, out_specs=out_specs, check_vma=False)
```

```python
import functools

import jax
import jax.numpy as jnp
from jax import lax
from jax.experimental import pallas as pl
from jax.experimental.pallas import tpu as pltpu
from jax.sharding import PartitionSpec as P

GELU_GAIN = 1.7015
RESIDUAL_SCALE = 0.2
BETA_BLOCK = 0.9805
BETA_TRANSITION = 0.9623
GROUP = 128
MESH = pl.DeviceIdType.MESH

TOP = 4
BOTTOM = 5


def activate(values):
    return GELU_GAIN * jax.nn.gelu(values, approximate=True)


def gather_kernel(nrow, ncol, img_ref, out_ref, send_sem, recv_sem, fwd_send, fwd_recv):
    s = lax.axis_index("section")
    r = lax.axis_index("row")
    c = lax.axis_index("col")
    n_img, th, tw = img_ref.shape[0], img_ref.shape[1], img_ref.shape[2]
    barrier = pltpu.get_barrier_semaphore()

    dests = []
    for i in range(n_img):
        is_self = jnp.logical_and(r == i, r == c)
        dests.append((i, jnp.logical_not(is_self), is_self))
    sources = []
    for cs in range(ncol):
        is_self = jnp.logical_and(c == r, cs == c)
        sources.append((cs, jnp.logical_not(is_self)))
    up = c - 1
    down = c + 1
    has_up = up >= 0
    has_down = down < ncol
    up_id = (s, r, lax.rem(up + ncol, ncol))
    down_id = (s, r, lax.rem(down, ncol))

    for i, is_remote, _ in dests:
        @pl.when(is_remote)
        def _():
            pl.semaphore_signal(barrier, 1, device_id=(s, i, r), device_id_type=MESH)
    for cs, is_remote in sources:
        @pl.when(is_remote)
        def _():
            pl.semaphore_signal(barrier, 1, device_id=(s, c, cs), device_id_type=MESH)
    for flag, dev in ((has_up, up_id), (has_down, down_id)):
        @pl.when(flag)
        def _():
            pl.semaphore_signal(barrier, 1, device_id=dev, device_id_type=MESH)
    peers = [p for _, p, _ in dests] + [p for _, p in sources] + [has_up, has_down]
    pl.semaphore_wait(barrier, sum(p.astype(jnp.int32) for p in peers))

    remote_copies = []
    for k in range(n_img):
        i = lax.rem(c + k, n_img)
        src = img_ref.at[i]
        dst = out_ref.at[pl.ds(TOP, th), c]
        rdesc = pltpu.make_async_remote_copy(
            src_ref=src,
            dst_ref=dst,
            send_sem=send_sem.at[k],
            recv_sem=recv_sem.at[c],
            device_id=(s, i, r),
            device_id_type=MESH,
        )
        is_self = jnp.logical_and(r == c, k == 0)
        is_remote = jnp.logical_not(is_self)

        @pl.when(is_remote)
        def _():
            rdesc.start()

        if k == 0:
            @pl.when(is_self)
            def _():
                pltpu.make_async_copy(src, dst, recv_sem.at[c]).start()

        remote_copies.append((rdesc, is_remote))

    forwards = []
    for k in range(ncol):
        cs = lax.rem(r - k + ncol, ncol)
        dst = out_ref.at[pl.ds(TOP, th), cs]
        pltpu.make_async_copy(dst, dst, recv_sem.at[cs]).wait()
        to_up = pltpu.make_async_remote_copy(
            src_ref=out_ref.at[pl.ds(TOP, BOTTOM), cs],
            dst_ref=out_ref.at[pl.ds(TOP + th, BOTTOM), cs],
            send_sem=fwd_send.at[0, k],
            recv_sem=fwd_recv.at[1, cs],
            device_id=up_id,
            device_id_type=MESH,
        )
        to_down = pltpu.make_async_remote_copy(
            src_ref=out_ref.at[pl.ds(th, TOP), cs],
            dst_ref=out_ref.at[pl.ds(0, TOP), cs],
            send_sem=fwd_send.at[1, k],
            recv_sem=fwd_recv.at[0, cs],
            device_id=down_id,
            device_id_type=MESH,
        )

        @pl.when(has_up)
        def _():
            to_up.start()

        @pl.when(has_down)
        def _():
            to_down.start()

        forwards.append((to_up, to_down, cs))

    for to_up, to_down, cs in forwards:
        @pl.when(has_down)
        def _():
            pltpu.make_async_copy(to_up.dst_ref, to_up.dst_ref, fwd_recv.at[1, cs]).wait()

        @pl.when(has_up)
        def _():
            pltpu.make_async_copy(to_down.dst_ref, to_down.dst_ref, fwd_recv.at[0, cs]).wait()

    for rdesc, is_remote in remote_copies:
        @pl.when(is_remote)
        def _():
            rdesc.wait_send()

    for to_up, to_down, cs in forwards:
        @pl.when(has_up)
        def _():
            to_up.wait_send()

        @pl.when(has_down)
        def _():
            to_down.wait_send()


def gather_strips(tiles, nrow, ncol):
    n_img, th, tw, ch = tiles.shape
    return pl.pallas_call(
        functools.partial(gather_kernel, nrow, ncol),
        out_shape=jax.ShapeDtypeStruct((TOP + th + BOTTOM, ncol, tw, ch), tiles.dtype),
        in_specs=[pl.BlockSpec(memory_space=pl.ANY)],
        out_specs=pl.BlockSpec(memory_space=pl.ANY),
        scratch_shapes=[
            pltpu.SemaphoreType.DMA((n_img,)),
            pltpu.SemaphoreType.DMA((ncol,)),
            pltpu.SemaphoreType.DMA((2, ncol)),
            pltpu.SemaphoreType.DMA((2, ncol)),
        ],
        compiler_params=pltpu.CompilerParams(collective_id=0, has_side_effects=True),
    )(tiles)


def inside_rows(count, width, first, height):
    rows = first + lax.broadcasted_iota(jnp.int32, (count * width, 1), 0) // width
    return jnp.logical_and(rows >= 0, rows < height)


def column_of(count, width):
    return lax.broadcasted_iota(jnp.int32, (count * width, 1), 0) % width


def conv_taps(rows_of, out_rows, width, w_ref, group):
    sl = slice(group * GROUP, (group + 1) * GROUP)
    slab = jnp.concatenate([rows_of(a)[:, :, sl] for a in range(3)], axis=-1)
    slab = slab.reshape(out_rows * width, 3 * GROUP).astype(jnp.bfloat16)
    taps = [
        jnp.concatenate([w_ref[(3 * a + b) * GROUP : (3 * a + b + 1) * GROUP, sl] for a in range(3)], axis=0)
        for b in range(3)
    ]
    y = jnp.dot(slab, jnp.concatenate(taps, axis=1), preferred_element_type=jnp.float32)
    return [y[:, b * GROUP : (b + 1) * GROUP] for b in range(3)]


def conv_same(x, w_ref):
    in_rows, width, channels = x.shape
    out_rows = in_rows - 2
    n = out_rows * width
    col = column_of(out_rows, width)
    outs = []
    for g in range(channels // GROUP):
        y = conv_taps(lambda a: x[a : a + out_rows], out_rows, width, w_ref, g)
        left = jnp.where(col == 0, 0.0, pltpu.roll(y[0], 1, 0))
        right = jnp.where(col == width - 1, 0.0, pltpu.roll(y[2], n - 1, 0))
        outs.append(y[1] + left + right)
    return jnp.concatenate(outs, axis=-1)


def block_body(base, height, x, win_ref, w1_ref, w2_ref, wout_ref):
    rows, width, ch = x.shape
    pre = (activate(x.reshape(rows * width, ch)) * BETA_BLOCK).astype(jnp.bfloat16)
    first = activate(jnp.dot(pre, win_ref[...], preferred_element_type=jnp.float32))
    first = jnp.where(inside_rows(rows, width, base, height), first, 0.0)
    first = first.astype(jnp.bfloat16).astype(jnp.float32).reshape(rows, width, -1)
    second = activate(conv_same(first, w1_ref))
    second = jnp.where(inside_rows(rows - 2, width, base + 1, height), second, 0.0)
    second = second.astype(jnp.bfloat16).astype(jnp.float32).reshape(rows - 2, width, -1)
    third = activate(conv_same(second, w2_ref)).astype(jnp.bfloat16)
    skip = x[2 : rows - 2].reshape((rows - 4) * width, ch)
    out = skip + RESIDUAL_SCALE * jnp.dot(third, wout_ref[...], preferred_element_type=jnp.float32)
    return out.astype(jnp.bfloat16)


def fused_kernel(base_ref, x_ref, bin_ref, b1_ref, b2_ref, bout_ref,
                 win_ref, w1_ref, w2_ref, wout_ref, wshort_ref, o_ref, pool_scr, sub_scr):
    in_rows, width, ch = x_ref.shape
    strip = x_ref[...].astype(jnp.float32)
    height = base_ref[1]
    block_result = block_body(base_ref[0], height, strip, bin_ref, b1_ref, b2_ref, bout_ref)
    rows = in_rows - 4
    core_rows = rows - 5
    half = width // 2
    base = base_ref[0] + 2
    x = block_result.astype(jnp.float32)
    pre = (activate(x) * BETA_TRANSITION).astype(jnp.bfloat16)

    core = pre.astype(jnp.float32).reshape(rows, width, ch)[2 : 2 + core_rows]
    core = core.reshape(core_rows // 2, 2, width, ch)
    summed = (core[:, 0] + core[:, 1]).reshape(core_rows // 2 * width, ch)
    n_pool = core_rows // 2 * half
    parts = []
    for k in range(ch // GROUP):
        pool_scr[k] = summed[:, k * GROUP : (k + 1) * GROUP]
        part = pool_scr.at[k]
        parts.append(part[pl.ds(0, n_pool, stride=2), :] + part[pl.ds(1, n_pool, stride=2), :])
    pooled = (jnp.concatenate(parts, axis=-1) * 0.25).astype(jnp.bfloat16)

    first = activate(jnp.dot(pre, win_ref[...], preferred_element_type=jnp.float32))
    first = jnp.where(inside_rows(rows, width, base, height), first, 0.0)
    first = first.astype(jnp.bfloat16).astype(jnp.float32).reshape(rows, width, -1)
    mid = first.shape[-1]
    first = jnp.concatenate([first, jnp.zeros((1, width, mid), jnp.float32)], axis=0)
    pairs = first.reshape((rows + 1) // 2, 2, width, mid)
    out_rows = (rows - 1) // 2
    picks = (pairs[:out_rows, 0], pairs[:out_rows, 1], pairs[1 : out_rows + 1, 0])
    n = out_rows * width
    col = column_of(out_rows, width)
    for g in range(mid // GROUP):
        y = conv_taps(lambda a: picks[a], out_rows, width, w1_ref, g)
        z = y[0] + pltpu.roll(y[1], n - 1, 0) + jnp.where(col >= width - 2, 0.0, pltpu.roll(y[2], n - 2, 0))
        sub_scr[g, pl.ds(0, n), :] = z
    picked = [sub_scr.at[g][pl.ds(0, out_rows * half, stride=2), :] for g in range(mid // GROUP)]
    second = activate(jnp.concatenate(picked, axis=-1))
    second = jnp.where(inside_rows(out_rows, half, base_ref[0] // 2 + 1, height // 2), second, 0.0)
    second = second.astype(jnp.bfloat16).astype(jnp.float32).reshape(out_rows, half, mid)
    third = activate(conv_same(second, w2_ref)).astype(jnp.bfloat16)
    out = jnp.dot(pooled, wshort_ref[...], preferred_element_type=jnp.float32)
    out = out + RESIDUAL_SCALE * jnp.dot(third, wout_ref[...], preferred_element_type=jnp.float32)
    o_ref[...] = out.astype(o_ref.dtype)


def vmem_call(kernel, out_shape, n_in, scratch=()):
    return pl.pallas_call(
        kernel,
        out_shape=out_shape,
        in_specs=[pl.BlockSpec(memory_space=pltpu.SMEM)] + [pl.BlockSpec(memory_space=pltpu.VMEM)] * n_in,
        out_specs=pl.BlockSpec(memory_space=pltpu.VMEM),
        scratch_shapes=list(scratch),
    )


def compute(strip, base_info, block_in, block_grouped_one, block_grouped_two, block_out,
            trans_in, trans_grouped_one, trans_grouped_two, trans_out, trans_short):
    in_rows, width, ch = strip.shape
    t_rows = in_rows - 4
    core_rows = t_rows - 5
    out_rows = (t_rows - 1) // 2
    mid = trans_in.shape[1]
    wide = trans_out.shape[1]
    scratch = (
        pltpu.VMEM((ch // GROUP, core_rows // 2 * width, GROUP), jnp.float32),
        pltpu.VMEM((mid // GROUP, out_rows * width + 8, GROUP), jnp.float32),
    )
    out_shape = jax.ShapeDtypeStruct(((core_rows // 2) * (width // 2), wide), jnp.bfloat16)
    features = vmem_call(fused_kernel, out_shape, 10, scratch)(
        base_info, strip, block_in, block_grouped_one, block_grouped_two, block_out,
        trans_in, trans_grouped_one, trans_grouped_two, trans_out, trans_short
    )
    return features.reshape(core_rows // 2, width // 2, wide)


def local(
    images,
    block_in,
    block_grouped_one,
    block_grouped_two,
    block_out,
    trans_in,
    trans_grouped_one,
    trans_grouped_two,
    trans_out,
    trans_short,
):
    nrow = lax.axis_size("row")
    ncol = lax.axis_size("col")
    _, n_img, th, tw, ch = images.shape
    c = lax.axis_index("col")
    base_info = jnp.stack([c * th - TOP, th * nrow]).astype(jnp.int32)
    tiles = images.reshape(n_img, th, tw * (ch // GROUP), GROUP)
    strip = gather_strips(tiles, nrow, ncol).reshape(TOP + th + BOTTOM, ncol * tw, ch)
    features = compute(strip, base_info, block_in, block_grouped_one, block_grouped_two, block_out,
                       trans_in, trans_grouped_one, trans_grouped_two, trans_out, trans_short)
    return features[None, None]


def solution(mesh):
    in_specs = (P("section", None, "row", "col", None), P(), P(), P(), P(), P(), P(), P(), P(), P())
    out_specs = P("section", "row", "col", None, None)
    return jax.shard_map(local, mesh=mesh, in_specs=in_specs, out_specs=out_specs, check_vma=False)
```

```python
import functools
import math

import jax
import jax.numpy as jnp
from jax import lax
from jax.experimental import pallas as pl
from jax.experimental.pallas import tpu as pltpu
from jax.sharding import PartitionSpec as P

GELU_GAIN = 1.7015
RESIDUAL_SCALE = 0.2
BETA_BLOCK = 0.9805
BETA_TRANSITION = 0.9623
GROUP = 128
MESH = pl.DeviceIdType.MESH
TANH_SCALE = math.sqrt(2.0 / math.pi)

TOP = 4
BOTTOM = 5


def activate(values, scale=1.0):
    inner = values * (TANH_SCALE + TANH_SCALE * 0.044715 * (values * values))
    half = values * (0.5 * GELU_GAIN * scale)
    return half + half * jnp.tanh(inner)


def gather_kernel(nrow, ncol, img_ref, out_ref, send_sem, recv_sem, fwd_send, fwd_recv):
    s = lax.axis_index("section")
    r = lax.axis_index("row")
    c = lax.axis_index("col")
    n_img, th, tw = img_ref.shape[0], img_ref.shape[1], img_ref.shape[2]
    barrier = pltpu.get_barrier_semaphore()

    dests = []
    for i in range(n_img):
        is_self = jnp.logical_and(r == i, r == c)
        dests.append((i, jnp.logical_not(is_self), is_self))
    sources = []
    for cs in range(ncol):
        is_self = jnp.logical_and(c == r, cs == c)
        sources.append((cs, jnp.logical_not(is_self)))
    up = c - 1
    down = c + 1
    has_up = up >= 0
    has_down = down < ncol
    up_id = (s, r, lax.rem(up + ncol, ncol))
    down_id = (s, r, lax.rem(down, ncol))

    for i, is_remote, _ in dests:
        @pl.when(is_remote)
        def _():
            pl.semaphore_signal(barrier, 1, device_id=(s, i, r), device_id_type=MESH)
    for cs, is_remote in sources:
        @pl.when(is_remote)
        def _():
            pl.semaphore_signal(barrier, 1, device_id=(s, c, cs), device_id_type=MESH)
    for flag, dev in ((has_up, up_id), (has_down, down_id)):
        @pl.when(flag)
        def _():
            pl.semaphore_signal(barrier, 1, device_id=dev, device_id_type=MESH)
    peers = [p for _, p, _ in dests] + [p for _, p in sources] + [has_up, has_down]
    pl.semaphore_wait(barrier, sum(p.astype(jnp.int32) for p in peers))

    remote_copies = []
    for k in range(n_img):
        i = lax.rem(c + k, n_img)
        src = img_ref.at[i]
        dst = out_ref.at[pl.ds(TOP, th), c]
        rdesc = pltpu.make_async_remote_copy(
            src_ref=src,
            dst_ref=dst,
            send_sem=send_sem.at[k],
            recv_sem=recv_sem.at[c],
            device_id=(s, i, r),
            device_id_type=MESH,
        )
        is_self = jnp.logical_and(r == c, k == 0)
        is_remote = jnp.logical_not(is_self)

        @pl.when(is_remote)
        def _():
            rdesc.start()

        if k == 0:
            @pl.when(is_self)
            def _():
                pltpu.make_async_copy(src, dst, recv_sem.at[c]).start()

        remote_copies.append((rdesc, is_remote))

    forwards = []
    for k in range(ncol):
        cs = lax.rem(r - k + ncol, ncol)
        dst = out_ref.at[pl.ds(TOP, th), cs]
        pltpu.make_async_copy(dst, dst, recv_sem.at[cs]).wait()
        to_up = pltpu.make_async_remote_copy(
            src_ref=out_ref.at[pl.ds(TOP, BOTTOM), cs],
            dst_ref=out_ref.at[pl.ds(TOP + th, BOTTOM), cs],
            send_sem=fwd_send.at[0, k],
            recv_sem=fwd_recv.at[1, cs],
            device_id=up_id,
            device_id_type=MESH,
        )
        to_down = pltpu.make_async_remote_copy(
            src_ref=out_ref.at[pl.ds(th, TOP), cs],
            dst_ref=out_ref.at[pl.ds(0, TOP), cs],
            send_sem=fwd_send.at[1, k],
            recv_sem=fwd_recv.at[0, cs],
            device_id=down_id,
            device_id_type=MESH,
        )

        @pl.when(has_up)
        def _():
            to_up.start()

        @pl.when(has_down)
        def _():
            to_down.start()

        forwards.append((to_up, to_down, cs))

    for to_up, to_down, cs in forwards:
        @pl.when(has_down)
        def _():
            pltpu.make_async_copy(to_up.dst_ref, to_up.dst_ref, fwd_recv.at[1, cs]).wait()

        @pl.when(has_up)
        def _():
            pltpu.make_async_copy(to_down.dst_ref, to_down.dst_ref, fwd_recv.at[0, cs]).wait()

    for rdesc, is_remote in remote_copies:
        @pl.when(is_remote)
        def _():
            rdesc.wait_send()

    for to_up, to_down, cs in forwards:
        @pl.when(has_up)
        def _():
            to_up.wait_send()

        @pl.when(has_down)
        def _():
            to_down.wait_send()


def gather_strips(tiles, nrow, ncol):
    n_img, th, tw, ch = tiles.shape
    return pl.pallas_call(
        functools.partial(gather_kernel, nrow, ncol),
        out_shape=jax.ShapeDtypeStruct((TOP + th + BOTTOM, ncol, tw, ch), tiles.dtype),
        in_specs=[pl.BlockSpec(memory_space=pl.ANY)],
        out_specs=pl.BlockSpec(memory_space=pl.ANY),
        scratch_shapes=[
            pltpu.SemaphoreType.DMA((n_img,)),
            pltpu.SemaphoreType.DMA((ncol,)),
            pltpu.SemaphoreType.DMA((2, ncol)),
            pltpu.SemaphoreType.DMA((2, ncol)),
        ],
        compiler_params=pltpu.CompilerParams(collective_id=0, has_side_effects=True),
    )(tiles)


def inside_rows(count, width, first, height):
    rows = first + lax.broadcasted_iota(jnp.int32, (count * width, 1), 0) // width
    return jnp.logical_and(rows >= 0, rows < height)


def column_of(count, width):
    return lax.broadcasted_iota(jnp.int32, (count * width, 1), 0) % width


def conv_taps(rows_of, out_rows, width, w_ref, group):
    sl = slice(group * GROUP, (group + 1) * GROUP)
    slab = jnp.concatenate([rows_of(a)[:, :, sl] for a in range(3)], axis=-1)
    slab = slab.reshape(out_rows * width, 3 * GROUP).astype(jnp.bfloat16)
    taps = [
        jnp.concatenate([w_ref[(3 * a + b) * GROUP : (3 * a + b + 1) * GROUP, sl] for a in range(3)], axis=0)
        for b in range(3)
    ]
    y = jnp.dot(slab, jnp.concatenate(taps, axis=1), preferred_element_type=jnp.float32)
    return [y[:, b * GROUP : (b + 1) * GROUP] for b in range(3)]


def conv_same(x, w_ref):
    in_rows, width, channels = x.shape
    out_rows = in_rows - 2
    n = out_rows * width
    col = column_of(out_rows, width)
    outs = []
    for g in range(channels // GROUP):
        y = conv_taps(lambda a: x[a : a + out_rows], out_rows, width, w_ref, g)
        left = jnp.where(col == 0, 0.0, pltpu.roll(y[0], 1, 0))
        right = jnp.where(col == width - 1, 0.0, pltpu.roll(y[2], n - 1, 0))
        outs.append(y[1] + left + right)
    return jnp.concatenate(outs, axis=-1)


def block_body(base, height, x, win_ref, w1_ref, w2_ref, wout_ref):
    rows, width, ch = x.shape
    pre = activate(x.reshape(rows * width, ch), BETA_BLOCK).astype(jnp.bfloat16)
    first = activate(jnp.dot(pre, win_ref[...], preferred_element_type=jnp.float32))
    first = jnp.where(inside_rows(rows, width, base, height), first, 0.0)
    first = first.astype(jnp.bfloat16).astype(jnp.float32).reshape(rows, width, -1)
    second = activate(conv_same(first, w1_ref))
    second = jnp.where(inside_rows(rows - 2, width, base + 1, height), second, 0.0)
    second = second.astype(jnp.bfloat16).astype(jnp.float32).reshape(rows - 2, width, -1)
    third = activate(conv_same(second, w2_ref)).astype(jnp.bfloat16)
    skip = x[2 : rows - 2].reshape((rows - 4) * width, ch)
    out = skip + RESIDUAL_SCALE * jnp.dot(third, wout_ref[...], preferred_element_type=jnp.float32)
    return out.astype(jnp.bfloat16)


def fused_kernel(base_ref, x_ref, bin_ref, b1_ref, b2_ref, bout_ref,
                 win_ref, w1_ref, w2_ref, wout_ref, wshort_ref, o_ref, pool_scr, sub_scr):
    in_rows, width, ch = x_ref.shape
    strip = x_ref[...].astype(jnp.float32)
    height = base_ref[1]
    block_result = block_body(base_ref[0], height, strip, bin_ref, b1_ref, b2_ref, bout_ref)
    rows = in_rows - 4
    core_rows = rows - 5
    half = width // 2
    base = base_ref[0] + 2
    x = block_result.astype(jnp.float32)
    pre = activate(x, BETA_TRANSITION).astype(jnp.bfloat16)

    core = pre.astype(jnp.float32).reshape(rows, width, ch)[2 : 2 + core_rows]
    core = core.reshape(core_rows // 2, 2, width, ch)
    summed = (core[:, 0] + core[:, 1]).reshape(core_rows // 2 * width, ch)
    n_pool = core_rows // 2 * half
    parts = []
    for k in range(ch // GROUP):
        pool_scr[k] = summed[:, k * GROUP : (k + 1) * GROUP]
        part = pool_scr.at[k]
        parts.append(part[pl.ds(0, n_pool, stride=2), :] + part[pl.ds(1, n_pool, stride=2), :])
    pooled = (jnp.concatenate(parts, axis=-1) * 0.25).astype(jnp.bfloat16)

    first = activate(jnp.dot(pre, win_ref[...], preferred_element_type=jnp.float32))
    first = jnp.where(inside_rows(rows, width, base, height), first, 0.0)
    first = first.astype(jnp.bfloat16).astype(jnp.float32).reshape(rows, width, -1)
    mid = first.shape[-1]
    first = jnp.concatenate([first, jnp.zeros((1, width, mid), jnp.float32)], axis=0)
    pairs = first.reshape((rows + 1) // 2, 2, width, mid)
    out_rows = (rows - 1) // 2
    picks = (pairs[:out_rows, 0], pairs[:out_rows, 1], pairs[1 : out_rows + 1, 0])
    n = out_rows * width
    col = column_of(out_rows, width)
    for g in range(mid // GROUP):
        y = conv_taps(lambda a: picks[a], out_rows, width, w1_ref, g)
        z = y[0] + pltpu.roll(y[1], n - 1, 0) + jnp.where(col >= width - 2, 0.0, pltpu.roll(y[2], n - 2, 0))
        sub_scr[g, pl.ds(0, n), :] = z
    picked = [sub_scr.at[g][pl.ds(0, out_rows * half, stride=2), :] for g in range(mid // GROUP)]
    second = activate(jnp.concatenate(picked, axis=-1))
    second = jnp.where(inside_rows(out_rows, half, base_ref[0] // 2 + 1, height // 2), second, 0.0)
    second = second.astype(jnp.bfloat16).astype(jnp.float32).reshape(out_rows, half, mid)
    third = activate(conv_same(second, w2_ref)).astype(jnp.bfloat16)
    out = jnp.dot(pooled, wshort_ref[...], preferred_element_type=jnp.float32)
    out = out + RESIDUAL_SCALE * jnp.dot(third, wout_ref[...], preferred_element_type=jnp.float32)
    o_ref[...] = out.astype(o_ref.dtype)


def vmem_call(kernel, out_shape, n_in, scratch=()):
    return pl.pallas_call(
        kernel,
        out_shape=out_shape,
        in_specs=[pl.BlockSpec(memory_space=pltpu.SMEM)] + [pl.BlockSpec(memory_space=pltpu.VMEM)] * n_in,
        out_specs=pl.BlockSpec(memory_space=pltpu.VMEM),
        scratch_shapes=list(scratch),
    )


def compute(strip, base_info, block_in, block_grouped_one, block_grouped_two, block_out,
            trans_in, trans_grouped_one, trans_grouped_two, trans_out, trans_short):
    in_rows, width, ch = strip.shape
    t_rows = in_rows - 4
    core_rows = t_rows - 5
    out_rows = (t_rows - 1) // 2
    mid = trans_in.shape[1]
    wide = trans_out.shape[1]
    scratch = (
        pltpu.VMEM((ch // GROUP, core_rows // 2 * width, GROUP), jnp.float32),
        pltpu.VMEM((mid // GROUP, out_rows * width + 8, GROUP), jnp.float32),
    )
    out_shape = jax.ShapeDtypeStruct(((core_rows // 2) * (width // 2), wide), jnp.bfloat16)
    features = vmem_call(fused_kernel, out_shape, 10, scratch)(
        base_info, strip, block_in, block_grouped_one, block_grouped_two, block_out,
        trans_in, trans_grouped_one, trans_grouped_two, trans_out, trans_short
    )
    return features.reshape(core_rows // 2, width // 2, wide)


def local(
    images,
    block_in,
    block_grouped_one,
    block_grouped_two,
    block_out,
    trans_in,
    trans_grouped_one,
    trans_grouped_two,
    trans_out,
    trans_short,
):
    nrow = lax.axis_size("row")
    ncol = lax.axis_size("col")
    _, n_img, th, tw, ch = images.shape
    c = lax.axis_index("col")
    base_info = jnp.stack([c * th - TOP, th * nrow]).astype(jnp.int32)
    tiles = images.reshape(n_img, th, tw * (ch // GROUP), GROUP)
    strip = gather_strips(tiles, nrow, ncol).reshape(TOP + th + BOTTOM, ncol * tw, ch)
    features = compute(strip, base_info, block_in, block_grouped_one, block_grouped_two, block_out,
                       trans_in, trans_grouped_one, trans_grouped_two, trans_out, trans_short)
    return features[None, None]


def solution(mesh):
    in_specs = (P("section", None, "row", "col", None), P(), P(), P(), P(), P(), P(), P(), P(), P())
    out_specs = P("section", "row", "col", None, None)
    return jax.shard_map(local, mesh=mesh, in_specs=in_specs, out_specs=out_specs, check_vma=False)
```

```python
import functools
import math

import jax
import jax.numpy as jnp
from jax import lax
from jax.experimental import pallas as pl
from jax.experimental.pallas import tpu as pltpu
from jax.sharding import PartitionSpec as P

GELU_GAIN = 1.7015
RESIDUAL_SCALE = 0.2
BETA_BLOCK = 0.9805
BETA_TRANSITION = 0.9623
GROUP = 128
MESH = pl.DeviceIdType.MESH
TANH_SCALE = math.sqrt(2.0 / math.pi)

TOP = 4
BOTTOM = 5


def activate(values, scale=1.0):
    inner = values * (TANH_SCALE + TANH_SCALE * 0.044715 * (values * values))
    half = values * (0.5 * GELU_GAIN * scale)
    return half + half * jnp.tanh(inner)


def gather_kernel(nrow, ncol, img_ref, out_ref, send_sem, recv_sem, fwd_send, fwd_recv):
    s = lax.axis_index("section")
    r = lax.axis_index("row")
    c = lax.axis_index("col")
    n_img, th, tw = img_ref.shape[0], img_ref.shape[1], img_ref.shape[2]
    barrier = pltpu.get_barrier_semaphore()

    dests = []
    for i in range(n_img):
        is_self = jnp.logical_and(r == i, r == c)
        dests.append((i, jnp.logical_not(is_self), is_self))
    sources = []
    for cs in range(ncol):
        is_self = jnp.logical_and(c == r, cs == c)
        sources.append((cs, jnp.logical_not(is_self)))
    up = c - 1
    down = c + 1
    has_up = up >= 0
    has_down = down < ncol
    up_id = (s, r, lax.rem(up + ncol, ncol))
    down_id = (s, r, lax.rem(down, ncol))

    for i, is_remote, _ in dests:
        @pl.when(is_remote)
        def _():
            pl.semaphore_signal(barrier, 1, device_id=(s, i, r), device_id_type=MESH)
    for cs, is_remote in sources:
        @pl.when(is_remote)
        def _():
            pl.semaphore_signal(barrier, 1, device_id=(s, c, cs), device_id_type=MESH)
    for flag, dev in ((has_up, up_id), (has_down, down_id)):
        @pl.when(flag)
        def _():
            pl.semaphore_signal(barrier, 1, device_id=dev, device_id_type=MESH)
    peers = [p for _, p, _ in dests] + [p for _, p in sources] + [has_up, has_down]
    pl.semaphore_wait(barrier, sum(p.astype(jnp.int32) for p in peers))

    remote_copies = []
    for k in range(n_img):
        i = lax.rem(c + k, n_img)
        src = img_ref.at[i]
        dst = out_ref.at[pl.ds(TOP, th), c]
        rdesc = pltpu.make_async_remote_copy(
            src_ref=src,
            dst_ref=dst,
            send_sem=send_sem.at[k],
            recv_sem=recv_sem.at[c],
            device_id=(s, i, r),
            device_id_type=MESH,
        )
        is_self = jnp.logical_and(r == c, k == 0)
        is_remote = jnp.logical_not(is_self)

        @pl.when(is_remote)
        def _():
            rdesc.start()

        if k == 0:
            @pl.when(is_self)
            def _():
                pltpu.make_async_copy(src, dst, recv_sem.at[c]).start()

        remote_copies.append((rdesc, is_remote))

    forwards = []
    for k in range(ncol):
        cs = lax.rem(r - k + ncol, ncol)
        dst = out_ref.at[pl.ds(TOP, th), cs]
        pltpu.make_async_copy(dst, dst, recv_sem.at[cs]).wait()
        to_up = pltpu.make_async_remote_copy(
            src_ref=out_ref.at[pl.ds(TOP, BOTTOM), cs],
            dst_ref=out_ref.at[pl.ds(TOP + th, BOTTOM), cs],
            send_sem=fwd_send.at[0, k],
            recv_sem=fwd_recv.at[1, cs],
            device_id=up_id,
            device_id_type=MESH,
        )
        to_down = pltpu.make_async_remote_copy(
            src_ref=out_ref.at[pl.ds(th, TOP), cs],
            dst_ref=out_ref.at[pl.ds(0, TOP), cs],
            send_sem=fwd_send.at[1, k],
            recv_sem=fwd_recv.at[0, cs],
            device_id=down_id,
            device_id_type=MESH,
        )

        @pl.when(has_up)
        def _():
            to_up.start()

        @pl.when(has_down)
        def _():
            to_down.start()

        forwards.append((to_up, to_down, cs))

    for to_up, to_down, cs in forwards:
        @pl.when(has_down)
        def _():
            pltpu.make_async_copy(to_up.dst_ref, to_up.dst_ref, fwd_recv.at[1, cs]).wait()

        @pl.when(has_up)
        def _():
            pltpu.make_async_copy(to_down.dst_ref, to_down.dst_ref, fwd_recv.at[0, cs]).wait()

    for rdesc, is_remote in remote_copies:
        @pl.when(is_remote)
        def _():
            rdesc.wait_send()

    for to_up, to_down, cs in forwards:
        @pl.when(has_up)
        def _():
            to_up.wait_send()

        @pl.when(has_down)
        def _():
            to_down.wait_send()


def gather_strips(tiles, nrow, ncol):
    n_img, th, tw, ch = tiles.shape
    return pl.pallas_call(
        functools.partial(gather_kernel, nrow, ncol),
        out_shape=jax.ShapeDtypeStruct((TOP + th + BOTTOM, ncol, tw, ch), tiles.dtype),
        in_specs=[pl.BlockSpec(memory_space=pl.ANY)],
        out_specs=pl.BlockSpec(memory_space=pl.ANY),
        scratch_shapes=[
            pltpu.SemaphoreType.DMA((n_img,)),
            pltpu.SemaphoreType.DMA((ncol,)),
            pltpu.SemaphoreType.DMA((2, ncol)),
            pltpu.SemaphoreType.DMA((2, ncol)),
        ],
        compiler_params=pltpu.CompilerParams(collective_id=0, has_side_effects=True),
    )(tiles)


def inside_rows(count, width, first, height):
    rows = first + lax.broadcasted_iota(jnp.int32, (count * width, 1), 0) // width
    return jnp.logical_and(rows >= 0, rows < height)


def column_of(count, width):
    return lax.broadcasted_iota(jnp.int32, (count * width, 1), 0) % width


def conv_taps(rows_of, out_rows, width, w_ref, group):
    sl = slice(group * GROUP, (group + 1) * GROUP)
    slab = jnp.concatenate([rows_of(a)[:, :, sl] for a in range(3)], axis=-1)
    slab = slab.reshape(out_rows * width, 3 * GROUP).astype(jnp.bfloat16)
    taps = [
        jnp.concatenate([w_ref[(3 * a + b) * GROUP : (3 * a + b + 1) * GROUP, sl] for a in range(3)], axis=0)
        for b in range(3)
    ]
    y = jnp.dot(slab, jnp.concatenate(taps, axis=1), preferred_element_type=jnp.float32)
    return [y[:, b * GROUP : (b + 1) * GROUP] for b in range(3)]


def conv_same(x, w_ref):
    in_rows, width, channels = x.shape
    out_rows = in_rows - 2
    n = out_rows * width
    col = column_of(out_rows, width)
    outs = []
    for g in range(channels // GROUP):
        y = conv_taps(lambda a: x[a : a + out_rows], out_rows, width, w_ref, g)
        left = jnp.where(col == 0, 0.0, pltpu.roll(y[0], 1, 0))
        right = jnp.where(col == width - 1, 0.0, pltpu.roll(y[2], n - 1, 0))
        outs.append(y[1] + left + right)
    return jnp.concatenate(outs, axis=-1)


def block_body(base, height, x, win_ref, w1_ref, w2_ref, wout_ref):
    rows, width, ch = x.shape
    pre = activate(x.reshape(rows * width, ch), BETA_BLOCK).astype(jnp.bfloat16)
    first = activate(jnp.dot(pre, win_ref[...], preferred_element_type=jnp.float32))
    first = jnp.where(inside_rows(rows, width, base, height), first, 0.0)
    first = first.astype(jnp.bfloat16).astype(jnp.float32).reshape(rows, width, -1)
    second = activate(conv_same(first, w1_ref))
    second = jnp.where(inside_rows(rows - 2, width, base + 1, height), second, 0.0)
    second = second.astype(jnp.bfloat16).astype(jnp.float32).reshape(rows - 2, width, -1)
    third = activate(conv_same(second, w2_ref)).astype(jnp.bfloat16)
    skip = x[2 : rows - 2].reshape((rows - 4) * width, ch)
    out = skip + RESIDUAL_SCALE * jnp.dot(third, wout_ref[...], preferred_element_type=jnp.float32)
    return out.astype(jnp.bfloat16)


def fused_kernel(base_ref, x_ref, bin_ref, b1_ref, b2_ref, bout_ref,
                 win_ref, w1_ref, w2_ref, wout_ref, wshort_ref, o_ref, pool_scr, sub_scr):
    in_rows, blocks, packed, lanes = x_ref.shape
    ch = bin_ref.shape[0]
    block_width = packed * lanes // ch
    width = blocks * block_width
    pieces = [x_ref[:, cb].astype(jnp.float32).reshape(in_rows, block_width, ch // lanes, lanes) for cb in range(blocks)]
    strip = jnp.concatenate([p.reshape(in_rows, block_width, ch) for p in pieces], axis=1)
    height = base_ref[1]
    block_result = block_body(base_ref[0], height, strip, bin_ref, b1_ref, b2_ref, bout_ref)
    rows = in_rows - 4
    core_rows = rows - 5
    half = width // 2
    base = base_ref[0] + 2
    x = block_result.astype(jnp.float32)
    pre = activate(x, BETA_TRANSITION).astype(jnp.bfloat16)

    core = pre.astype(jnp.float32).reshape(rows, width, ch)[2 : 2 + core_rows]
    core = core.reshape(core_rows // 2, 2, width, ch)
    summed = (core[:, 0] + core[:, 1]).reshape(core_rows // 2 * width, ch)
    n_pool = core_rows // 2 * half
    parts = []
    for k in range(ch // GROUP):
        pool_scr[k] = summed[:, k * GROUP : (k + 1) * GROUP]
        part = pool_scr.at[k]
        parts.append(part[pl.ds(0, n_pool, stride=2), :] + part[pl.ds(1, n_pool, stride=2), :])
    pooled = (jnp.concatenate(parts, axis=-1) * 0.25).astype(jnp.bfloat16)

    first = activate(jnp.dot(pre, win_ref[...], preferred_element_type=jnp.float32))
    first = jnp.where(inside_rows(rows, width, base, height), first, 0.0)
    first = first.astype(jnp.bfloat16).astype(jnp.float32).reshape(rows, width, -1)
    mid = first.shape[-1]
    first = jnp.concatenate([first, jnp.zeros((1, width, mid), jnp.float32)], axis=0)
    pairs = first.reshape((rows + 1) // 2, 2, width, mid)
    out_rows = (rows - 1) // 2
    picks = (pairs[:out_rows, 0], pairs[:out_rows, 1], pairs[1 : out_rows + 1, 0])
    n = out_rows * width
    col = column_of(out_rows, width)
    for g in range(mid // GROUP):
        y = conv_taps(lambda a: picks[a], out_rows, width, w1_ref, g)
        z = y[0] + pltpu.roll(y[1], n - 1, 0) + jnp.where(col >= width - 2, 0.0, pltpu.roll(y[2], n - 2, 0))
        sub_scr[g, pl.ds(0, n), :] = z
    picked = [sub_scr.at[g][pl.ds(0, out_rows * half, stride=2), :] for g in range(mid // GROUP)]
    second = activate(jnp.concatenate(picked, axis=-1))
    second = jnp.where(inside_rows(out_rows, half, base_ref[0] // 2 + 1, height // 2), second, 0.0)
    second = second.astype(jnp.bfloat16).astype(jnp.float32).reshape(out_rows, half, mid)
    third = activate(conv_same(second, w2_ref)).astype(jnp.bfloat16)
    out = jnp.dot(pooled, wshort_ref[...], preferred_element_type=jnp.float32)
    out = out + RESIDUAL_SCALE * jnp.dot(third, wout_ref[...], preferred_element_type=jnp.float32)
    o_ref[...] = out.astype(o_ref.dtype)


def vmem_call(kernel, out_shape, n_in, scratch=()):
    return pl.pallas_call(
        kernel,
        out_shape=out_shape,
        in_specs=[pl.BlockSpec(memory_space=pltpu.SMEM)] + [pl.BlockSpec(memory_space=pltpu.VMEM)] * n_in,
        out_specs=pl.BlockSpec(memory_space=pltpu.VMEM),
        scratch_shapes=list(scratch),
    )


def compute(strip, base_info, block_in, block_grouped_one, block_grouped_two, block_out,
            trans_in, trans_grouped_one, trans_grouped_two, trans_out, trans_short):
    in_rows, blocks, packed, lanes = strip.shape
    ch = block_in.shape[0]
    width = blocks * packed * lanes // ch
    t_rows = in_rows - 4
    core_rows = t_rows - 5
    out_rows = (t_rows - 1) // 2
    mid = trans_in.shape[1]
    wide = trans_out.shape[1]
    scratch = (
        pltpu.VMEM((ch // GROUP, core_rows // 2 * width, GROUP), jnp.float32),
        pltpu.VMEM((mid // GROUP, out_rows * width + 8, GROUP), jnp.float32),
    )
    out_shape = jax.ShapeDtypeStruct(((core_rows // 2) * (width // 2), wide), jnp.bfloat16)
    features = vmem_call(fused_kernel, out_shape, 10, scratch)(
        base_info, strip, block_in, block_grouped_one, block_grouped_two, block_out,
        trans_in, trans_grouped_one, trans_grouped_two, trans_out, trans_short
    )
    return features.reshape(core_rows // 2, width // 2, wide)


def local(
    images,
    block_in,
    block_grouped_one,
    block_grouped_two,
    block_out,
    trans_in,
    trans_grouped_one,
    trans_grouped_two,
    trans_out,
    trans_short,
):
    nrow = lax.axis_size("row")
    ncol = lax.axis_size("col")
    _, n_img, th, tw, ch = images.shape
    c = lax.axis_index("col")
    base_info = jnp.stack([c * th - TOP, th * nrow]).astype(jnp.int32)
    tiles = images.reshape(n_img, th, tw * (ch // GROUP), GROUP)
    strip = gather_strips(tiles, nrow, ncol)
    features = compute(strip, base_info, block_in, block_grouped_one, block_grouped_two, block_out,
                       trans_in, trans_grouped_one, trans_grouped_two, trans_out, trans_short)
    return features[None, None]


def solution(mesh):
    in_specs = (P("section", None, "row", "col", None), P(), P(), P(), P(), P(), P(), P(), P(), P())
    out_specs = P("section", "row", "col", None, None)
    return jax.shard_map(local, mesh=mesh, in_specs=in_specs, out_specs=out_specs, check_vma=False)
```

```python
import functools
import math

import jax
import jax.numpy as jnp
from jax import lax
from jax.experimental import pallas as pl
from jax.experimental.pallas import tpu as pltpu
from jax.sharding import PartitionSpec as P

GELU_GAIN = 1.7015
RESIDUAL_SCALE = 0.2
BETA_BLOCK = 0.9805
BETA_TRANSITION = 0.9623
GROUP = 128
MESH = pl.DeviceIdType.MESH
TANH_SCALE = math.sqrt(2.0 / math.pi)

TOP = 4
BOTTOM = 5


def activate(values, scale=1.0):
    inner = values * (TANH_SCALE + TANH_SCALE * 0.044715 * (values * values))
    half = values * (0.5 * GELU_GAIN * scale)
    return half + half * jnp.tanh(inner)


def gather_kernel(nrow, ncol, img_ref, out_ref, send_sem, recv_sem, fwd_send, fwd_recv):
    s = lax.axis_index("section")
    r = lax.axis_index("row")
    c = lax.axis_index("col")
    n_img, th, tw = img_ref.shape[0], img_ref.shape[1], img_ref.shape[2]
    barrier = pltpu.get_barrier_semaphore()

    dests = []
    for i in range(n_img):
        is_self = jnp.logical_and(r == i, r == c)
        dests.append((i, jnp.logical_not(is_self), is_self))
    sources = []
    for cs in range(ncol):
        is_self = jnp.logical_and(c == r, cs == c)
        sources.append((cs, jnp.logical_not(is_self)))
    up = c - 1
    down = c + 1
    has_up = up >= 0
    has_down = down < ncol
    up_id = (s, r, lax.rem(up + ncol, ncol))
    down_id = (s, r, lax.rem(down, ncol))

    for i, is_remote, _ in dests:
        @pl.when(is_remote)
        def _():
            pl.semaphore_signal(barrier, 1, device_id=(s, i, r), device_id_type=MESH)
    for cs, is_remote in sources:
        @pl.when(is_remote)
        def _():
            pl.semaphore_signal(barrier, 1, device_id=(s, c, cs), device_id_type=MESH)
    for flag, dev in ((has_up, up_id), (has_down, down_id)):
        @pl.when(flag)
        def _():
            pl.semaphore_signal(barrier, 1, device_id=dev, device_id_type=MESH)
    peers = [p for _, p, _ in dests] + [p for _, p in sources] + [has_up, has_down]
    pl.semaphore_wait(barrier, sum(p.astype(jnp.int32) for p in peers))

    remote_copies = []
    for k in range(n_img):
        i = lax.rem(c + k, n_img)
        src = img_ref.at[i]
        dst = out_ref.at[pl.ds(TOP, th), c]
        rdesc = pltpu.make_async_remote_copy(
            src_ref=src,
            dst_ref=dst,
            send_sem=send_sem.at[k],
            recv_sem=recv_sem.at[c],
            device_id=(s, i, r),
            device_id_type=MESH,
        )
        is_self = jnp.logical_and(r == c, k == 0)
        is_remote = jnp.logical_not(is_self)

        @pl.when(is_remote)
        def _():
            rdesc.start()

        if k == 0:
            @pl.when(is_self)
            def _():
                pltpu.make_async_copy(src, dst, recv_sem.at[c]).start()

        remote_copies.append((rdesc, is_remote))

    forwards = []
    for k in range(ncol):
        cs = lax.rem(r - k + ncol, ncol)
        dst = out_ref.at[pl.ds(TOP, th), cs]
        pltpu.make_async_copy(dst, dst, recv_sem.at[cs]).wait()
        to_up = pltpu.make_async_remote_copy(
            src_ref=out_ref.at[pl.ds(TOP, BOTTOM), cs],
            dst_ref=out_ref.at[pl.ds(TOP + th, BOTTOM), cs],
            send_sem=fwd_send.at[0, k],
            recv_sem=fwd_recv.at[1, cs],
            device_id=up_id,
            device_id_type=MESH,
        )
        to_down = pltpu.make_async_remote_copy(
            src_ref=out_ref.at[pl.ds(th, TOP), cs],
            dst_ref=out_ref.at[pl.ds(0, TOP), cs],
            send_sem=fwd_send.at[1, k],
            recv_sem=fwd_recv.at[0, cs],
            device_id=down_id,
            device_id_type=MESH,
        )

        @pl.when(has_up)
        def _():
            to_up.start()

        @pl.when(has_down)
        def _():
            to_down.start()

        forwards.append((to_up, to_down, cs))

    for to_up, to_down, cs in forwards:
        @pl.when(has_down)
        def _():
            pltpu.make_async_copy(to_up.dst_ref, to_up.dst_ref, fwd_recv.at[1, cs]).wait()

        @pl.when(has_up)
        def _():
            pltpu.make_async_copy(to_down.dst_ref, to_down.dst_ref, fwd_recv.at[0, cs]).wait()

    for rdesc, is_remote in remote_copies:
        @pl.when(is_remote)
        def _():
            rdesc.wait_send()

    for to_up, to_down, cs in forwards:
        @pl.when(has_up)
        def _():
            to_up.wait_send()

        @pl.when(has_down)
        def _():
            to_down.wait_send()


def gather_strips(tiles, nrow, ncol):
    n_img, th, tw, ch = tiles.shape
    return pl.pallas_call(
        functools.partial(gather_kernel, nrow, ncol),
        out_shape=jax.ShapeDtypeStruct((TOP + th + BOTTOM, ncol, tw, ch), tiles.dtype),
        in_specs=[pl.BlockSpec(memory_space=pl.ANY)],
        out_specs=pl.BlockSpec(memory_space=pl.ANY),
        scratch_shapes=[
            pltpu.SemaphoreType.DMA((n_img,)),
            pltpu.SemaphoreType.DMA((ncol,)),
            pltpu.SemaphoreType.DMA((2, ncol)),
            pltpu.SemaphoreType.DMA((2, ncol)),
        ],
        compiler_params=pltpu.CompilerParams(collective_id=0, has_side_effects=True),
    )(tiles)


def inside_rows(count, width, first, height):
    rows = first + lax.broadcasted_iota(jnp.int32, (count * width, 1), 0) // width
    return jnp.logical_and(rows >= 0, rows < height)


def column_of(count, width):
    return lax.broadcasted_iota(jnp.int32, (count * width, 1), 0) % width


def conv_taps(rows_of, out_rows, width, w_ref, group):
    sl = slice(group * GROUP, (group + 1) * GROUP)
    slab = jnp.concatenate([rows_of(a)[:, :, sl] for a in range(3)], axis=-1)
    slab = slab.reshape(out_rows * width, 3 * GROUP).astype(jnp.bfloat16)
    taps = [
        jnp.concatenate([w_ref[(3 * a + b) * GROUP : (3 * a + b + 1) * GROUP, sl] for a in range(3)], axis=0)
        for b in range(3)
    ]
    y = jnp.dot(slab, jnp.concatenate(taps, axis=1), preferred_element_type=jnp.float32)
    return [y[:, b * GROUP : (b + 1) * GROUP] for b in range(3)]


def conv_same(x, w_ref):
    in_rows, width, channels = x.shape
    out_rows = in_rows - 2
    n = out_rows * width
    col = column_of(out_rows, width)
    outs = []
    for g in range(channels // GROUP):
        y = conv_taps(lambda a: x[a : a + out_rows], out_rows, width, w_ref, g)
        left = jnp.where(col == 0, 0.0, pltpu.roll(y[0], 1, 0))
        right = jnp.where(col == width - 1, 0.0, pltpu.roll(y[2], n - 1, 0))
        outs.append(y[1] + left + right)
    return jnp.concatenate(outs, axis=-1)


def block_body(base, height, x, win_ref, w1_ref, w2_ref, wout_ref):
    rows, width, ch = x.shape
    pre = activate(x.reshape(rows * width, ch), BETA_BLOCK).astype(jnp.bfloat16)
    first = activate(jnp.dot(pre, win_ref[...], preferred_element_type=jnp.float32))
    first = jnp.where(inside_rows(rows, width, base, height), first, 0.0)
    first = first.astype(jnp.bfloat16).astype(jnp.float32).reshape(rows, width, -1)
    second = activate(conv_same(first, w1_ref))
    second = jnp.where(inside_rows(rows - 2, width, base + 1, height), second, 0.0)
    second = second.astype(jnp.bfloat16).astype(jnp.float32).reshape(rows - 2, width, -1)
    third = activate(conv_same(second, w2_ref)).astype(jnp.bfloat16)
    skip = x[2 : rows - 2].reshape((rows - 4) * width, ch)
    out = skip + RESIDUAL_SCALE * jnp.dot(third, wout_ref[...], preferred_element_type=jnp.float32)
    return out.astype(jnp.bfloat16)


def fused_kernel(x_ref, bin_ref, b1_ref, b2_ref, bout_ref,
                 win_ref, w1_ref, w2_ref, wout_ref, wshort_ref, o_ref, pool_scr, sub_scr):
    in_rows, blocks, packed, lanes = x_ref.shape
    ch = bin_ref.shape[0]
    block_width = packed * lanes // ch
    width = blocks * block_width
    pieces = [x_ref[:, cb].astype(jnp.float32).reshape(in_rows, block_width, ch // lanes, lanes) for cb in range(blocks)]
    strip = jnp.concatenate([p.reshape(in_rows, block_width, ch) for p in pieces], axis=1)
    th = in_rows - TOP - BOTTOM
    height = th * lax.axis_size("row")
    start = lax.axis_index("col") * th - TOP
    block_result = block_body(start, height, strip, bin_ref, b1_ref, b2_ref, bout_ref)
    rows = in_rows - 4
    core_rows = rows - 5
    half = width // 2
    base = start + 2
    x = block_result.astype(jnp.float32)
    pre = activate(x, BETA_TRANSITION).astype(jnp.bfloat16)

    core = pre.astype(jnp.float32).reshape(rows, width, ch)[2 : 2 + core_rows]
    core = core.reshape(core_rows // 2, 2, width, ch)
    summed = (core[:, 0] + core[:, 1]).reshape(core_rows // 2 * width, ch)
    n_pool = core_rows // 2 * half
    parts = []
    for k in range(ch // GROUP):
        pool_scr[k] = summed[:, k * GROUP : (k + 1) * GROUP]
        part = pool_scr.at[k]
        parts.append(part[pl.ds(0, n_pool, stride=2), :] + part[pl.ds(1, n_pool, stride=2), :])
    pooled = (jnp.concatenate(parts, axis=-1) * 0.25).astype(jnp.bfloat16)

    first = activate(jnp.dot(pre, win_ref[...], preferred_element_type=jnp.float32))
    first = jnp.where(inside_rows(rows, width, base, height), first, 0.0)
    first = first.astype(jnp.bfloat16).astype(jnp.float32).reshape(rows, width, -1)
    mid = first.shape[-1]
    first = jnp.concatenate([first, jnp.zeros((1, width, mid), jnp.float32)], axis=0)
    pairs = first.reshape((rows + 1) // 2, 2, width, mid)
    out_rows = (rows - 1) // 2
    picks = (pairs[:out_rows, 0], pairs[:out_rows, 1], pairs[1 : out_rows + 1, 0])
    n = out_rows * width
    col = column_of(out_rows, width)
    for g in range(mid // GROUP):
        y = conv_taps(lambda a: picks[a], out_rows, width, w1_ref, g)
        z = y[0] + pltpu.roll(y[1], n - 1, 0) + jnp.where(col >= width - 2, 0.0, pltpu.roll(y[2], n - 2, 0))
        sub_scr[g, pl.ds(0, n), :] = z
    picked = [sub_scr.at[g][pl.ds(0, out_rows * half, stride=2), :] for g in range(mid // GROUP)]
    second = activate(jnp.concatenate(picked, axis=-1))
    second = jnp.where(inside_rows(out_rows, half, (start + TOP) // 2 - 1, height // 2), second, 0.0)
    second = second.astype(jnp.bfloat16).astype(jnp.float32).reshape(out_rows, half, mid)
    third = activate(conv_same(second, w2_ref)).astype(jnp.bfloat16)
    out = jnp.dot(pooled, wshort_ref[...], preferred_element_type=jnp.float32)
    out = out + RESIDUAL_SCALE * jnp.dot(third, wout_ref[...], preferred_element_type=jnp.float32)
    o_ref[...] = out.astype(o_ref.dtype)


def vmem_call(kernel, out_shape, n_in, scratch=()):
    return pl.pallas_call(
        kernel,
        out_shape=out_shape,
        in_specs=[pl.BlockSpec(memory_space=pltpu.VMEM)] * n_in,
        out_specs=pl.BlockSpec(memory_space=pltpu.VMEM),
        scratch_shapes=list(scratch),
    )


def compute(strip, block_in, block_grouped_one, block_grouped_two, block_out,
            trans_in, trans_grouped_one, trans_grouped_two, trans_out, trans_short):
    in_rows, blocks, packed, lanes = strip.shape
    ch = block_in.shape[0]
    width = blocks * packed * lanes // ch
    t_rows = in_rows - 4
    core_rows = t_rows - 5
    out_rows = (t_rows - 1) // 2
    mid = trans_in.shape[1]
    wide = trans_out.shape[1]
    scratch = (
        pltpu.VMEM((ch // GROUP, core_rows // 2 * width, GROUP), jnp.float32),
        pltpu.VMEM((mid // GROUP, out_rows * width + 8, GROUP), jnp.float32),
    )
    out_shape = jax.ShapeDtypeStruct(((core_rows // 2) * (width // 2), wide), jnp.bfloat16)
    features = vmem_call(fused_kernel, out_shape, 10, scratch)(
        strip, block_in, block_grouped_one, block_grouped_two, block_out,
        trans_in, trans_grouped_one, trans_grouped_two, trans_out, trans_short
    )
    return features.reshape(core_rows // 2, width // 2, wide)


def local(
    images,
    block_in,
    block_grouped_one,
    block_grouped_two,
    block_out,
    trans_in,
    trans_grouped_one,
    trans_grouped_two,
    trans_out,
    trans_short,
):
    nrow = lax.axis_size("row")
    ncol = lax.axis_size("col")
    _, n_img, th, tw, ch = images.shape
    tiles = images.reshape(n_img, th, tw * (ch // GROUP), GROUP)
    strip = gather_strips(tiles, nrow, ncol)
    features = compute(strip, block_in, block_grouped_one, block_grouped_two, block_out,
                       trans_in, trans_grouped_one, trans_grouped_two, trans_out, trans_short)
    return features[None, None]


def solution(mesh):
    in_specs = (P("section", None, "row", "col", None), P(), P(), P(), P(), P(), P(), P(), P(), P())
    out_specs = P("section", "row", "col", None, None)
    return jax.shard_map(local, mesh=mesh, in_specs=in_specs, out_specs=out_specs, check_vma=False)
```

```python
import functools
import math

import jax
import jax.numpy as jnp
from jax import lax
from jax.experimental import pallas as pl
from jax.experimental.pallas import tpu as pltpu
from jax.sharding import PartitionSpec as P

GELU_GAIN = 1.7015
RESIDUAL_SCALE = 0.2
BETA_BLOCK = 0.9805
BETA_TRANSITION = 0.9623
GROUP = 128
MESH = pl.DeviceIdType.MESH
TANH_SCALE = math.sqrt(2.0 / math.pi)

TOP = 4
BOTTOM = 5


def activate(values, scale=1.0):
    inner = values * (TANH_SCALE + TANH_SCALE * 0.044715 * (values * values))
    half = values * (0.5 * GELU_GAIN * scale)
    return half + half * jnp.tanh(inner)


def gather_kernel(nrow, ncol, img_ref, out_ref, send_sem, recv_sem, fwd_send, fwd_recv):
    s = lax.axis_index("section")
    r = lax.axis_index("row")
    c = lax.axis_index("col")
    n_img, th, tw = img_ref.shape[0], img_ref.shape[1], img_ref.shape[2]
    barrier = pltpu.get_barrier_semaphore()

    dests = []
    for i in range(n_img):
        is_self = jnp.logical_and(r == i, r == c)
        dests.append((i, jnp.logical_not(is_self), is_self))
    sources = []
    for cs in range(ncol):
        is_self = jnp.logical_and(c == r, cs == c)
        sources.append((cs, jnp.logical_not(is_self)))
    up = c - 1
    down = c + 1
    has_up = up >= 0
    has_down = down < ncol
    up_id = (s, r, lax.rem(up + ncol, ncol))
    down_id = (s, r, lax.rem(down, ncol))

    for i, is_remote, _ in dests:
        @pl.when(is_remote)
        def _():
            pl.semaphore_signal(barrier, 1, device_id=(s, i, r), device_id_type=MESH)
    for cs, is_remote in sources:
        @pl.when(is_remote)
        def _():
            pl.semaphore_signal(barrier, 1, device_id=(s, c, cs), device_id_type=MESH)
    for flag, dev in ((has_up, up_id), (has_down, down_id)):
        @pl.when(flag)
        def _():
            pl.semaphore_signal(barrier, 1, device_id=dev, device_id_type=MESH)
    peers = [p for _, p, _ in dests] + [p for _, p in sources] + [has_up, has_down]
    pl.semaphore_wait(barrier, sum(p.astype(jnp.int32) for p in peers))

    remote_copies = []
    for k in range(n_img):
        i = lax.rem(c + k, n_img)
        src = img_ref.at[i]
        dst = out_ref.at[pl.ds(TOP, th), c]
        rdesc = pltpu.make_async_remote_copy(
            src_ref=src,
            dst_ref=dst,
            send_sem=send_sem.at[k],
            recv_sem=recv_sem.at[c],
            device_id=(s, i, r),
            device_id_type=MESH,
        )
        is_self = jnp.logical_and(r == c, k == 0)
        is_remote = jnp.logical_not(is_self)

        @pl.when(is_remote)
        def _():
            rdesc.start()

        if k == 0:
            @pl.when(is_self)
            def _():
                pltpu.make_async_copy(src, dst, recv_sem.at[c]).start()

        remote_copies.append((rdesc, is_remote))

    forwards = []
    for k in range(ncol):
        cs = lax.rem(r - k + ncol, ncol)
        dst = out_ref.at[pl.ds(TOP, th), cs]
        pltpu.make_async_copy(dst, dst, recv_sem.at[cs]).wait()
        to_up = pltpu.make_async_remote_copy(
            src_ref=out_ref.at[pl.ds(TOP, BOTTOM), cs],
            dst_ref=out_ref.at[pl.ds(TOP + th, BOTTOM), cs],
            send_sem=fwd_send.at[0, k],
            recv_sem=fwd_recv.at[1, cs],
            device_id=up_id,
            device_id_type=MESH,
        )
        to_down = pltpu.make_async_remote_copy(
            src_ref=out_ref.at[pl.ds(th, TOP), cs],
            dst_ref=out_ref.at[pl.ds(0, TOP), cs],
            send_sem=fwd_send.at[1, k],
            recv_sem=fwd_recv.at[0, cs],
            device_id=down_id,
            device_id_type=MESH,
        )

        @pl.when(has_up)
        def _():
            to_up.start()

        @pl.when(has_down)
        def _():
            to_down.start()

        forwards.append((to_up, to_down, cs))

    for to_up, to_down, cs in forwards:
        @pl.when(has_down)
        def _():
            pltpu.make_async_copy(to_up.dst_ref, to_up.dst_ref, fwd_recv.at[1, cs]).wait()

        @pl.when(has_up)
        def _():
            pltpu.make_async_copy(to_down.dst_ref, to_down.dst_ref, fwd_recv.at[0, cs]).wait()

    for rdesc, is_remote in remote_copies:
        @pl.when(is_remote)
        def _():
            rdesc.wait_send()

    for to_up, to_down, cs in forwards:
        @pl.when(has_up)
        def _():
            to_up.wait_send()

        @pl.when(has_down)
        def _():
            to_down.wait_send()


def gather_strips(tiles, nrow, ncol):
    n_img, th, tw, ch = tiles.shape
    return pl.pallas_call(
        functools.partial(gather_kernel, nrow, ncol),
        out_shape=jax.ShapeDtypeStruct((TOP + th + BOTTOM, ncol, tw, ch), tiles.dtype),
        in_specs=[pl.BlockSpec(memory_space=pl.ANY)],
        out_specs=pl.BlockSpec(memory_space=pl.ANY),
        scratch_shapes=[
            pltpu.SemaphoreType.DMA((n_img,)),
            pltpu.SemaphoreType.DMA((ncol,)),
            pltpu.SemaphoreType.DMA((2, ncol)),
            pltpu.SemaphoreType.DMA((2, ncol)),
        ],
        compiler_params=pltpu.CompilerParams(collective_id=0, has_side_effects=True),
    )(tiles)


def inside_rows(count, width, first, height):
    rows = first + lax.broadcasted_iota(jnp.int32, (count * width, 1), 0) // width
    return jnp.logical_and(rows >= 0, rows < height)


def column_of(count, width):
    return lax.broadcasted_iota(jnp.int32, (count * width, 1), 0) % width


def conv_taps(rows_of, out_rows, width, w_ref, group):
    sl = slice(group * GROUP, (group + 1) * GROUP)
    slab = jnp.concatenate([rows_of(a)[:, :, sl] for a in range(3)], axis=-1)
    slab = slab.reshape(out_rows * width, 3 * GROUP).astype(jnp.bfloat16)
    taps = [
        jnp.concatenate([w_ref[(3 * a + b) * GROUP : (3 * a + b + 1) * GROUP, sl] for a in range(3)], axis=0)
        for b in range(3)
    ]
    y = jnp.dot(slab, jnp.concatenate(taps, axis=1), preferred_element_type=jnp.float32)
    return [y[:, b * GROUP : (b + 1) * GROUP] for b in range(3)]


def conv_same(x, w_ref):
    in_rows, width, channels = x.shape
    out_rows = in_rows - 2
    n = out_rows * width
    col = column_of(out_rows, width)
    outs = []
    for g in range(channels // GROUP):
        y = conv_taps(lambda a: x[a : a + out_rows], out_rows, width, w_ref, g)
        left = jnp.where(col == 0, 0.0, pltpu.roll(y[0], 1, 0))
        right = jnp.where(col == width - 1, 0.0, pltpu.roll(y[2], n - 1, 0))
        outs.append(y[1] + left + right)
    return jnp.concatenate(outs, axis=-1)


def block_body(base, height, x, win_ref, w1_ref, w2_ref, wout_ref):
    rows, width, ch = x.shape
    pre = activate(x.reshape(rows * width, ch), BETA_BLOCK).astype(jnp.bfloat16)
    first = activate(jnp.dot(pre, win_ref[...], preferred_element_type=jnp.float32))
    first = jnp.where(inside_rows(rows, width, base, height), first, 0.0)
    first = first.astype(jnp.bfloat16).astype(jnp.float32).reshape(rows, width, -1)
    second = activate(conv_same(first, w1_ref))
    second = jnp.where(inside_rows(rows - 2, width, base + 1, height), second, 0.0)
    second = second.astype(jnp.bfloat16).astype(jnp.float32).reshape(rows - 2, width, -1)
    third = activate(conv_same(second, w2_ref)).astype(jnp.bfloat16)
    skip = x[2 : rows - 2].reshape((rows - 4) * width, ch)
    out = skip + RESIDUAL_SCALE * jnp.dot(third, wout_ref[...], preferred_element_type=jnp.float32)
    return out.astype(jnp.bfloat16)


def fused_kernel(x_ref, bin_ref, b1_ref, b2_ref, bout_ref,
                 win_ref, w1_ref, w2_ref, wout_ref, wshort_ref, o_ref, pool_scr, sub_scr):
    in_rows, blocks, packed, lanes = x_ref.shape
    ch = bin_ref.shape[0]
    block_width = packed * lanes // ch
    width = blocks * block_width
    pieces = [x_ref[:, cb].astype(jnp.float32).reshape(in_rows, block_width, ch // lanes, lanes) for cb in range(blocks)]
    strip = jnp.concatenate([p.reshape(in_rows, block_width, ch) for p in pieces], axis=1)
    th = in_rows - TOP - BOTTOM
    height = th * lax.axis_size("row")
    start = lax.axis_index("col") * th - TOP
    block_result = block_body(start, height, strip, bin_ref, b1_ref, b2_ref, bout_ref)
    rows = in_rows - 4
    core_rows = rows - 5
    half = width // 2
    base = start + 2
    x = block_result.astype(jnp.float32)
    pre = activate(x, BETA_TRANSITION).astype(jnp.bfloat16)

    core = pre.astype(jnp.float32).reshape(rows, width, ch)[2 : 2 + core_rows]
    core = core.reshape(core_rows // 2, 2, width, ch)
    summed = (core[:, 0] + core[:, 1]).reshape(core_rows // 2 * width, ch)
    n_pool = core_rows // 2 * half
    parts = []
    for k in range(ch // GROUP):
        pool_scr[k] = summed[:, k * GROUP : (k + 1) * GROUP]
        part = pool_scr.at[k]
        parts.append(part[pl.ds(0, n_pool, stride=2), :] + part[pl.ds(1, n_pool, stride=2), :])
    pooled = (jnp.concatenate(parts, axis=-1) * 0.25).astype(jnp.bfloat16)

    first = activate(jnp.dot(pre, win_ref[...], preferred_element_type=jnp.float32))
    first = jnp.where(inside_rows(rows, width, base, height), first, 0.0)
    first = first.astype(jnp.bfloat16).astype(jnp.float32).reshape(rows, width, -1)
    mid = first.shape[-1]
    first = first.reshape(rows * width, mid)
    out_rows = (rows - 1) // 2
    n = out_rows * half
    col = column_of(out_rows, half)
    outs = []
    for g in range(mid // GROUP):
        sl = slice(g * GROUP, (g + 1) * GROUP)
        sub_scr[g, pl.ds(0, rows * width), :] = first[:, sl]
        sub_scr[g, pl.ds(rows * width, width), :] = jnp.zeros((width, GROUP), jnp.float32)
        planes = [
            sub_scr.at[g][pl.ds(p, (rows + 1) * half, stride=2), :].reshape((rows + 1) // 2, 2, half, GROUP)
            for p in range(2)
        ]
        slabs = [
            jnp.concatenate([q[:out_rows, 0], q[:out_rows, 1], q[1 : out_rows + 1, 0]], axis=-1)
            .reshape(n, 3 * GROUP)
            .astype(jnp.bfloat16)
            for q in planes
        ]
        taps = [
            jnp.concatenate([w1_ref[(3 * a + b) * GROUP : (3 * a + b + 1) * GROUP, sl] for a in range(3)], axis=0)
            for b in range(3)
        ]
        ye = jnp.dot(slabs[0], jnp.concatenate([taps[0], taps[2]], axis=1), preferred_element_type=jnp.float32)
        yo = jnp.dot(slabs[1], taps[1], preferred_element_type=jnp.float32)
        right = jnp.where(col == half - 1, 0.0, pltpu.roll(ye[:, GROUP:], n - 1, 0))
        outs.append(ye[:, :GROUP] + yo + right)
    second = activate(jnp.concatenate(outs, axis=-1))
    second = jnp.where(inside_rows(out_rows, half, (start + TOP) // 2 - 1, height // 2), second, 0.0)
    second = second.astype(jnp.bfloat16).astype(jnp.float32).reshape(out_rows, half, mid)
    third = activate(conv_same(second, w2_ref)).astype(jnp.bfloat16)
    out = jnp.dot(pooled, wshort_ref[...], preferred_element_type=jnp.float32)
    out = out + RESIDUAL_SCALE * jnp.dot(third, wout_ref[...], preferred_element_type=jnp.float32)
    o_ref[...] = out.astype(o_ref.dtype)


def vmem_call(kernel, out_shape, n_in, scratch=()):
    return pl.pallas_call(
        kernel,
        out_shape=out_shape,
        in_specs=[pl.BlockSpec(memory_space=pltpu.VMEM)] * n_in,
        out_specs=pl.BlockSpec(memory_space=pltpu.VMEM),
        scratch_shapes=list(scratch),
    )


def compute(strip, block_in, block_grouped_one, block_grouped_two, block_out,
            trans_in, trans_grouped_one, trans_grouped_two, trans_out, trans_short):
    in_rows, blocks, packed, lanes = strip.shape
    ch = block_in.shape[0]
    width = blocks * packed * lanes // ch
    t_rows = in_rows - 4
    core_rows = t_rows - 5
    out_rows = (t_rows - 1) // 2
    mid = trans_in.shape[1]
    wide = trans_out.shape[1]
    scratch = (
        pltpu.VMEM((ch // GROUP, core_rows // 2 * width, GROUP), jnp.float32),
        pltpu.VMEM((mid // GROUP, (t_rows + 1) * width, GROUP), jnp.float32),
    )
    out_shape = jax.ShapeDtypeStruct(((core_rows // 2) * (width // 2), wide), jnp.bfloat16)
    features = vmem_call(fused_kernel, out_shape, 10, scratch)(
        strip, block_in, block_grouped_one, block_grouped_two, block_out,
        trans_in, trans_grouped_one, trans_grouped_two, trans_out, trans_short
    )
    return features.reshape(core_rows // 2, width // 2, wide)


def local(
    images,
    block_in,
    block_grouped_one,
    block_grouped_two,
    block_out,
    trans_in,
    trans_grouped_one,
    trans_grouped_two,
    trans_out,
    trans_short,
):
    nrow = lax.axis_size("row")
    ncol = lax.axis_size("col")
    _, n_img, th, tw, ch = images.shape
    tiles = images.reshape(n_img, th, tw * (ch // GROUP), GROUP)
    strip = gather_strips(tiles, nrow, ncol)
    features = compute(strip, block_in, block_grouped_one, block_grouped_two, block_out,
                       trans_in, trans_grouped_one, trans_grouped_two, trans_out, trans_short)
    return features[None, None]


def solution(mesh):
    in_specs = (P("section", None, "row", "col", None), P(), P(), P(), P(), P(), P(), P(), P(), P())
    out_specs = P("section", "row", "col", None, None)
    return jax.shard_map(local, mesh=mesh, in_specs=in_specs, out_specs=out_specs, check_vma=False)
```
